128 devices in a mesh: fsdp: 16 (over y_lo, z, core), chan: 8 (over y_hi, x).
Axes of the slice: x: 4, y: 4 (y_hi: 2, y_lo: 2; y = y_hi * 2 + y_lo), z: 4, core: 2. Of those that a mesh axis runs over, the one named last changes fastest.
Arguments:
- in_master: float32 [4096, 2, 4096], P(('fsdp', 'chan')), may hold values from -0.09375 to 0.09375
- in_moment: float32 [4096, 2, 4096], P(('fsdp', 'chan')), may hold values from -1.8 to 1.8
- in_velocity: float32 [4096, 2, 4096], P(('fsdp', 'chan')), may hold values from 0.05 to 1
- in_grad: bfloat16 [4096, 2, 4096], P(('fsdp', 'chan')), may hold values from -6 to 6
- out_master: float32 [4096, 4096], P(('fsdp', 'chan')), may hold values from -0.09375 to 0.09375
- out_moment: float32 [4096, 4096], P(('fsdp', 'chan')), may hold values from -1.8 to 1.8
- out_velocity: float32 [4096, 4096], P(('fsdp', 'chan')), may hold values from 0.001 to 1
- out_grad: bfloat16 [4096, 4096], P(('fsdp', 'chan')), may hold values from -6 to 6
- embed_table: bfloat16 [65536, 4096], P('fsdp', 'chan'), may hold values from -18 to 18
- tokens: int32 [4, 2048], P(None, 'fsdp'), may hold values from 0 to 65535, as said below
- conv_state: bfloat16 [2048, 3, 4096], P('fsdp', None, 'chan'), may hold values from -6 to 6
- ssm_state: float32 [2048, 16, 4096], P('fsdp', None, 'chan'), may hold values from -6 to 6
- conv_weight: float32 [4, 4096], P(None, 'chan'), may hold values from -3 to 3
- conv_bias: float32 [4096], P('chan'), may hold values from -3 to 3
- x_proj_w: bfloat16 [288, 4096], P(None, 'chan'), may hold values from -0.09375 to 0.09375
- dt_proj_w: bfloat16 [4096, 256], P('chan'), may hold values from -0.375 to 0.375
- dt_bias: float32 [4096], P('chan'), may hold values from -4.5 to -2
- a_log: float32 [16, 4096], P(None, 'chan'), may hold values from 0 to 2.77
- d_skip: float32 [4096], P('chan'), may hold values from 0.5 to 2
Outputs:
- in_master_new: float32 [4096, 2, 4096], P(('fsdp', 'chan'))
- out_master_new: float32 [4096, 4096], P(('fsdp', 'chan'))
- block_out: bfloat16 [4, 2048, 4096], P(None, 'fsdp', 'chan')
- conv_state_new: bfloat16 [2048, 3, 4096], P('fsdp', None, 'chan')
- ssm_state_new: float32 [2048, 16, 4096], P('fsdp', None, 'chan')
The draws below stay inside these ranges and needn't reach their ends.
Inputs may be any that keep to these rules, and one draw needn't show every extreme that they name: Split the ids into 16 equal consecutive vocabulary blocks and the sequences into 16 equal consecutive replicas; of one replica's 4 x 128 tokens at most 64 lie in any one block, and some block holds exactly 64 of them.
All inputs are finite; a program needn't handle non-finite values.
Results may differ from the reference program's by a relative error of at most 0.012.
Values may be sent and summed in bfloat16 or wider, within the bound.
No kernel may reach another device: no remote copies, remote signals or barrier semaphores. Data moves between devices by JAX's collectives and lax.ppermute only.
A program may use at most 128 MiB of HBM per device.

```python
import math
import jax
import jax.numpy as jnp
from jax import lax

D = 4096
DI = 4096
RANK = 256
NSTATE = 16
KERNEL = 4
VOCAB = 65536
STEPS = 4
ROWS = 128
ALLROWS = 2048
CAP = 64
N_CHAN = 8


def draw_embed_table(key, part):
    keys = jax.random.split(jax.random.fold_in(key, 17), 3)
    row_scale = jnp.exp(jax.random.uniform(keys[0], (VOCAB, 1), jnp.float32, math.log(0.2), math.log(2.0)))
    col_scale = jnp.exp(jax.random.uniform(keys[1], (1, D), jnp.float32, math.log(0.3), math.log(3.0)))
    base = jnp.clip(jax.random.normal(keys[2], (VOCAB, D), jnp.float32), -3.0, 3.0)
    return (base * row_scale * col_scale).astype(jnp.bfloat16)


def draw_tokens(key, part):
    base = jax.random.fold_in(key, 29)
    replicas = ALLROWS // ROWS
    count = STEPS * ROWS
    block_ids = VOCAB // replicas
    slots = replicas * CAP

    def one_replica(inner_key):
        keys = jax.random.split(inner_key, 4)
        scores = jax.random.permutation(keys[0], slots).astype(jnp.int32)
        full_block = jax.random.randint(keys[1], (), 0, replicas, jnp.int32)
        slot_block = (jnp.arange(slots, dtype=jnp.int32) // CAP).astype(jnp.int32)
        scores = jnp.where(slot_block == full_block, scores - slots, scores)
        chosen = jnp.argsort(scores, stable=True)[:count].astype(jnp.int32)
        chosen = jax.random.permutation(keys[2], chosen)
        owner = chosen // CAP
        within = jax.random.randint(keys[3], (count,), 0, block_ids, jnp.int32)
        return (owner * block_ids + within).astype(jnp.int32)
    every = jax.vmap(one_replica)(jax.random.split(base, replicas))
    return jnp.transpose(every.reshape(replicas, STEPS, ROWS), (1, 0, 2)).reshape(STEPS, ALLROWS).astype(jnp.int32)


def steps_of(stream_key, extent, shards, low, top_value):
    def one(axis_at, shards_of):
        draws = jax.random.uniform(jax.random.fold_in(jax.random.fold_in(stream_key, 6), axis_at), (shards_of,), jnp.float32, low / len(shards), top_value / len(shards))
        return jnp.repeat(jnp.exp(draws), extent[axis_at] // shards_of).reshape((-1,) + (1,) * (len(extent) - axis_at - 1))

    level = one(*shards[0])
    for cut in shards[1:]:
        level = level * one(*cut)
    return level


def normal_values(key, extent, spread, bound, pieces=(), kind=jnp.bfloat16):
    entries = jax.random.normal(key, extent, jnp.float32) * spread
    if len(pieces) > 0:
        entries = steps_of(key, extent, pieces, -0.22, 0.18) * entries
    return jnp.clip(entries, min=-bound, max=bound).astype(kind)


def setup_inputs(seed: int = 0) -> dict:
    splits = jax.random.split(jax.random.key(seed), 20)
    in_master = normal_values(splits[0], (D, 2, DI), D ** -0.5, 0.09375, ((0, 128),), jnp.float32)
    in_moment = normal_values(splits[1], (D, 2, DI), 0.3, 1.8, ((0, 128),), jnp.float32)
    in_velocity = jnp.clip(jnp.exp(math.log(1.0) - 2.9957323 * jax.random.uniform(splits[2], (D, 2, DI), jnp.float32) ** steps_of(splits[2], (D, 2, DI), ((0, 128),), -0.2, 0.2)), 0.05, 1.0)
    in_grad = normal_values(splits[3], (D, 2, DI), 1.0, 6.0, ((0, 128),))
    out_master = normal_values(splits[4], (D, DI), DI ** -0.5, 0.09375, ((0, 128),), jnp.float32)
    out_moment = normal_values(splits[5], (D, DI), 0.3, 1.8, ((0, 128),), jnp.float32)
    out_velocity = jnp.clip(jnp.exp(math.log(1.0) - 6.9077552 * jax.random.uniform(splits[6], (D, DI), jnp.float32) ** steps_of(splits[6], (D, DI), ((0, 128),), -0.2, 0.2)), 0.001, 1.0)
    out_grad = normal_values(splits[7], (D, DI), 1.0, 6.0, ((0, 128),))
    embed_table = draw_embed_table(jax.random.fold_in(splits[19], 71), 0)
    tokens = draw_tokens(jax.random.fold_in(splits[19], 71), 0)
    conv_state = normal_values(splits[10], (ALLROWS, KERNEL - 1, DI), 1.0, 6.0, ((0, 16), (2, 8)))
    ssm_state = normal_values(splits[11], (ALLROWS, NSTATE, DI), 1.0, 6.0, ((0, 16), (2, 8)), jnp.float32)
    conv_weight = normal_values(splits[12], (KERNEL, DI), KERNEL ** -0.5, 3.0, ((1, 8),), jnp.float32)
    conv_bias = normal_values(splits[13], (DI,), 0.5, 3.0, ((0, 8),), jnp.float32)
    x_proj_w = normal_values(splits[14], (RANK + 2 * NSTATE, DI), DI ** -0.5, 0.09375, ((1, 8),))
    dt_proj_w = normal_values(splits[15], (DI, RANK), RANK ** -0.5, 0.375, ((0, 8),))
    dt_bias = jnp.clip(-4.5 + 2.5 * jax.random.uniform(splits[16], (DI,), jnp.float32) ** steps_of(splits[16], (DI,), ((0, 8),), -0.2, 0.2), -4.5, -2.0)
    a_log = jnp.clip(2.77 * jax.random.uniform(splits[17], (NSTATE, DI), jnp.float32) ** steps_of(splits[17], (NSTATE, DI), ((1, 8),), -0.2, 0.2), 0.0, 2.77)
    d_skip = jnp.clip(0.5 + 1.5 * jax.random.uniform(splits[18], (DI,), jnp.float32) ** steps_of(splits[18], (DI,), ((0, 8),), -0.2, 0.2), 0.5, 2.0)
    return {"in_master": in_master, "in_moment": in_moment, "in_velocity": in_velocity, "in_grad": in_grad, "out_master": out_master, "out_moment": out_moment, "out_velocity": out_velocity, "out_grad": out_grad, "embed_table": embed_table, "tokens": tokens, "conv_state": conv_state, "ssm_state": ssm_state, "conv_weight": conv_weight, "conv_bias": conv_bias, "x_proj_w": x_proj_w, "dt_proj_w": dt_proj_w, "dt_bias": dt_bias, "a_log": a_log, "d_skip": d_skip}


learn_rate = 0.01
beta_first = 0.8
beta_second = 0.95
adam_eps = 1e-08
weight_decay = 0.1
bias_first = 1.0 - math.pow(0.8, 10)
bias_second = 1.0 - math.pow(0.95, 10)
norm_eps = 1e-06

def adam_update(master, moment, velocity, grad):
    gradient = grad.astype(jnp.float32)
    moment = beta_first * moment + (1.0 - beta_first) * gradient
    velocity = beta_second * velocity + (1.0 - beta_second) * gradient * gradient
    update = moment / bias_first / (jnp.sqrt(velocity / bias_second) + adam_eps)
    return master - learn_rate * (update + weight_decay * master)

def reference(in_master, in_moment, in_velocity, in_grad, out_master, out_moment, out_velocity, out_grad, embed_table, tokens, conv_state, ssm_state, conv_weight, conv_bias, x_proj_w, dt_proj_w, dt_bias, a_log, d_skip):
    in_new = adam_update(in_master, in_moment, in_velocity, in_grad)
    out_new = adam_update(out_master, out_moment, out_velocity, out_grad)
    relay_x = in_new[:, 0, :].astype(jnp.bfloat16)
    relay_z = in_new[:, 1, :].astype(jnp.bfloat16)
    relay_out = out_new.astype(jnp.bfloat16)
    inputs = embed_table[tokens]
    steps, rows = tokens.shape
    flat = inputs.reshape(steps * rows, D).astype(jnp.float32)
    normed = (flat * lax.rsqrt(lax.optimization_barrier(jnp.mean(flat * flat, axis=1, keepdims=True)) + norm_eps)).astype(jnp.bfloat16)
    x_in = jnp.dot(normed, relay_x, preferred_element_type=jnp.float32).astype(jnp.bfloat16).reshape(steps, rows, DI)
    z_in = jnp.dot(normed, relay_z, preferred_element_type=jnp.float32).astype(jnp.bfloat16).reshape(steps, rows, DI)
    decay = -jnp.exp(a_log)
    group_width = DI // N_CHAN
    weight_groups = relay_out.reshape(D, N_CHAN, group_width).astype(jnp.float32)
    window_state = conv_state
    state = ssm_state
    outputs = []
    for step in range(steps):
        window = jnp.concatenate([window_state, x_in[step][:, None, :]], axis=1)
        mixed_conv = lax.optimization_barrier(jnp.sum(window.astype(jnp.float32) * conv_weight[None], axis=1)) + conv_bias
        act = jax.nn.silu(mixed_conv).astype(jnp.bfloat16)
        dbc = jnp.dot(act, x_proj_w.T, preferred_element_type=jnp.float32)
        dt_low = dbc[:, :RANK].astype(jnp.bfloat16)
        b_mat = dbc[:, RANK:RANK + NSTATE]
        c_mat = dbc[:, RANK + NSTATE:]
        delta = jax.nn.softplus(jnp.dot(dt_low, dt_proj_w.T, preferred_element_type=jnp.float32) + dt_bias)
        act_real = act.astype(jnp.float32)
        state = jnp.exp(delta[:, None, :] * decay[None]) * state + (delta * act_real)[:, None, :] * b_mat[:, :, None]
        y_out = lax.optimization_barrier(jnp.sum(c_mat[:, :, None] * state, axis=1)) + d_skip * act_real
        gated = (y_out * jax.nn.silu(z_in[step].astype(jnp.float32))).astype(jnp.bfloat16)
        gated_groups = gated.reshape(rows, N_CHAN, group_width).astype(jnp.float32)
        partials = jnp.einsum('rgk,dgk->grd', gated_groups, weight_groups, precision=lax.Precision.HIGHEST)
        partials = lax.optimization_barrier(partials.astype(jnp.bfloat16))
        mixed = lax.optimization_barrier(jnp.sum(partials.astype(jnp.float32), axis=0))
        outputs.append((inputs[step].astype(jnp.float32) + mixed).astype(jnp.bfloat16))
        window_state = window[:, 1:, :]
    return (in_new, out_new, jnp.stack(outputs), window_state, state)
```

```python
import functools
import math

import jax
import jax.numpy as jnp
from jax import lax
from jax.experimental import pallas as pl
from jax.experimental.pallas import tpu as pltpu
from jax.sharding import PartitionSpec as P

RANK = 256
NSTATE = 16

learn_rate = 0.01
beta_first = 0.8
beta_second = 0.95
adam_eps = 1e-08
weight_decay = 0.1
bias_first = 1.0 - math.pow(0.8, 10)
bias_second = 1.0 - math.pow(0.95, 10)
norm_eps = 1e-06

BOTH = ("fsdp", "chan")
DEVICES = [
    (yl, z, co, yh, x)
    for yl in range(2)
    for z in range(4)
    for co in range(2)
    for yh in range(2)
    for x in range(4)
]


def place_of(yl, z, co, yh, x):
    return (yl * 8 + z * 2 + co) * 8 + yh * 4 + x


def in_route(k):
    return [
        (place_of(yl, z, co, yh, x), place_of(yh, z, co, yl, (x + k) % 4))
        for yl, z, co, yh, x in DEVICES
    ]


def out_route(j):
    return [
        (place_of(yl, z, co, yh, x), place_of(yl, x, co, (yh + j) % 2, z))
        for yl, z, co, yh, x in DEVICES
    ]


def from_x(a, k):
    return lax.ppermute(a, "chan", [(i, (i // 4) * 4 + (i % 4 - k) % 4) for i in range(8)])


def from_partner(a):
    return lax.ppermute(a, "chan", [(i, i ^ 4) for i in range(8)])


def adam_update(master, moment, velocity, grad):
    gradient = grad.astype(jnp.float32)
    moment = beta_first * moment + (1.0 - beta_first) * gradient
    velocity = beta_second * velocity + (1.0 - beta_second) * gradient * gradient
    update = moment / bias_first / (jnp.sqrt(velocity / bias_second) + adam_eps)
    return master - learn_rate * (update + weight_decay * master)


def in_product_kernel(s_ref, a0, a1, a2, a3, w0, w1, o_ref, acc):
    k = pl.program_id(0)
    for kk, a in enumerate((a0, a1, a2, a3)):

        @pl.when(k == kk)
        def _(kk=kk, a=a):
            total = None
            for h, w in enumerate((w0, w1)):
                lhs = jnp.concatenate(
                    [a[:, h * 128 : h * 128 + 128], a[:, 256 + h * 128 : 384 + h * 128]], axis=1
                )
                part = jnp.dot(lhs, w[...].reshape(256, 512), preferred_element_type=jnp.float32)
                total = part if total is None else total + part
            if kk == 0:
                acc[...] = total
            elif kk < 3:
                acc[...] += total
            else:
                o_ref[...] = (acc[...] + total).astype(o_ref.dtype)


def in_product(chunks, weights, column, x, dtype):
    tokens = chunks[0].shape[0]
    scalars = jnp.stack([column, x]).astype(jnp.int32)
    whole = pl.BlockSpec((tokens, 512), lambda k, s: (0, 0))
    return pl.pallas_call(
        in_product_kernel,
        out_shape=jax.ShapeDtypeStruct((tokens, 512), dtype),
        grid_spec=pltpu.PrefetchScalarGridSpec(
            num_scalar_prefetch=1,
            grid=(4,),
            in_specs=[whole] * 4
            + [
                pl.BlockSpec((2, 128, 512), lambda k, s: (lax.rem(s[1] + k, 4), 0, s[0])),
                pl.BlockSpec((2, 128, 512), lambda k, s: (4 + lax.rem(s[1] + k, 4), 0, s[0])),
            ],
            out_specs=whole,
            scratch_shapes=[pltpu.VMEM((tokens, 512), jnp.float32)],
        ),
        compiler_params=pltpu.CompilerParams(vmem_limit_bytes=24 * 2**20),
        cost_estimate=pl.CostEstimate(
            flops=2 * tokens * 2048 * 512, bytes_accessed=6 * 2**20, transcendentals=0
        ),
        name="in_product",
    )(scalars, *chunks, weights, weights)


def out_product_kernel(s_ref, a0, a1, a2, a3, w_ref, o_ref, acc):
    k = pl.program_id(0)
    rows = [
        w_ref[xs * 2 + co, yh * 32 : yh * 32 + 32, :]
        for co in range(2)
        for yh in range(2)
        for xs in range(4)
    ]
    rhs = jnp.concatenate(rows, axis=0)
    for kk, a in enumerate((a0, a1, a2, a3)):

        @pl.when(k == kk)
        def _(kk=kk, a=a):
            total = lax.dot_general(
                a[...], rhs, (((1,), (1,)), ((), ())), preferred_element_type=jnp.float32
            )
            if kk == 0:
                acc[...] = total
            elif kk < 3:
                acc[...] += total
            else:
                o_ref[...] = (acc[...] + total).astype(o_ref.dtype)


def out_product(chunks, weights, block, x, dtype):
    tokens = chunks[0].shape[0]
    scalars = jnp.stack([block, x]).astype(jnp.int32)
    whole = pl.BlockSpec((tokens, 512), lambda k, s: (0, 0))

    def where(k, s):
        source = lax.rem(s[1] + k, 4)
        return (s[0], 2 + source // 2, lax.rem(source, 2))

    return pl.pallas_call(
        out_product_kernel,
        out_shape=jax.ShapeDtypeStruct((tokens, 512), dtype),
        grid_spec=pltpu.PrefetchScalarGridSpec(
            num_scalar_prefetch=1,
            grid=(4,),
            in_specs=[whole] * 4 + [pl.BlockSpec((8, 64, 512), where)],
            out_specs=whole,
            scratch_shapes=[pltpu.VMEM((tokens, 512), jnp.float32)],
        ),
        compiler_params=pltpu.CompilerParams(vmem_limit_bytes=24 * 2**20),
        cost_estimate=pl.CostEstimate(
            flops=2 * tokens * 2048 * 512, bytes_accessed=6 * 2**20, transcendentals=0
        ),
        name="out_product",
    )(scalars, *chunks, weights)


def per_device(
    in_master,
    in_moment,
    in_velocity,
    in_grad,
    out_master,
    out_moment,
    out_velocity,
    out_grad,
    embed_table,
    tokens,
    conv_state,
    ssm_state,
    conv_weight,
    conv_bias,
    x_proj_w,
    dt_proj_w,
    dt_bias,
    a_log,
    d_skip,
):
    bf16 = jnp.bfloat16
    f32 = jnp.float32
    chan = lax.axis_index("chan")
    yh, x = chan // 4, chan % 4
    replicas = lax.axis_size("fsdp")
    vocab_rows, feature_part = embed_table.shape
    steps, rows = tokens.shape
    count = steps * rows
    capacity = 2 * count // replicas

    flat_tokens = tokens.reshape(count)
    owner = flat_tokens // vocab_rows
    order = jnp.arange(count, dtype=jnp.int32)
    before = jnp.logical_and(owner[:, None] == owner[None, :], order[:, None] < order[None, :])
    slot = jnp.sum(before.astype(jnp.int32), axis=0)
    place = owner * capacity + slot
    slots = jnp.arange(replicas * capacity, dtype=jnp.int32)
    hit = place[None, :] == slots[:, None]
    requests = jnp.sum(jnp.where(hit, flat_tokens[None, :] + 1, 0), axis=1) - 1
    asked = lax.all_to_all(
        requests.reshape(replicas, capacity), "fsdp", split_axis=0, concat_axis=0, tiled=True
    )

    in_new = adam_update(in_master, in_moment, in_velocity, in_grad)
    out_new = adam_update(out_master, out_moment, out_velocity, out_grad)
    own = in_new.shape[0]

    def route_in(matrix):
        blocks = in_new[:, matrix, :].astype(bf16).reshape(own, 2, 4, 512)
        got = []
        for k in range(4):
            piece = lax.dynamic_index_in_dim(blocks, (x + k) % 4, 2, keepdims=False)
            got.append(lax.ppermute(piece.reshape(own, 1024), BOTH, in_route(k)))
        stacked = jnp.stack(got)
        return jnp.concatenate(
            [lax.dynamic_index_in_dim(stacked, (x - source) % 4, 0, keepdims=False) for source in range(4)],
            axis=0,
        )

    def route_out():
        halves = out_new.astype(bf16).reshape(own, 2, 2048)
        got = []
        for j in range(2):
            piece = lax.dynamic_index_in_dim(halves, (yh + j) % 2, 1, keepdims=False)
            got.append(lax.ppermute(piece, BOTH, out_route(j)))
        first = jnp.where(yh == 0, got[0], got[1])
        second = jnp.where(yh == 0, got[1], got[0])
        both = jnp.concatenate([first, second], axis=0)
        return jnp.concatenate([both[:, :1024], both[:, 1024:]], axis=0)

    weights_x = lax.all_gather(route_in(0), "fsdp", axis=0, tiled=False)
    rest = jnp.concatenate([route_in(1), route_out()], axis=0)
    weights_zo = lax.all_gather(rest, "fsdp", axis=0, tiled=False)

    offset = jnp.clip(asked - lax.axis_index("fsdp") * vocab_rows, 0, vocab_rows - 1)
    looked = embed_table.at[offset.reshape(-1)].get(mode="promise_in_bounds")
    replies = lax.all_to_all(
        looked.reshape(replicas, capacity, feature_part), "fsdp", split_axis=0, concat_axis=0, tiled=True
    )
    found = replies.reshape(replicas * capacity, feature_part).at[place].get(mode="promise_in_bounds")

    chunks = [found] + [from_x(found, k) for k in (1, 2, 3)]
    found_real = found.astype(f32)
    squares = jnp.sum(found_real * found_real, axis=1).reshape(steps, rows)
    everyone = lax.all_to_all(
        jnp.broadcast_to(squares[None], (8, steps, rows)), "chan", 0, 0, tiled=True
    )
    scale = lax.rsqrt(everyone.sum(axis=0) / (8 * feature_part) + norm_eps)

    def project(weights):
        away = from_partner(in_product(chunks, weights, 1 - yh, x, bf16))
        here = in_product(chunks, weights, yh, x, f32)
        total = (here + away.astype(f32)).reshape(steps, rows, -1)
        return (total * scale[:, :, None]).astype(bf16)

    x_in = project(weights_x)

    window = jnp.concatenate([conv_state, jnp.moveaxis(x_in, 0, 1)], axis=1)
    acts = []
    for step in range(steps):
        mixed_conv = (
            jnp.sum(window[:, step : step + 4].astype(f32) * conv_weight[None], axis=1) + conv_bias
        )
        acts.append(jax.nn.silu(mixed_conv).astype(bf16))
    window_state = window[:, steps:, :]
    act = jnp.concatenate(acts, axis=0)
    contract_last = (((1,), (1,)), ((), ()))
    partial_value = lax.dot_general(act, x_proj_w, contract_last, preferred_element_type=f32).astype(bf16)
    arrived = lax.all_to_all(
        jnp.broadcast_to(partial_value[None], (8, *partial_value.shape)), "chan", 0, 0, tiled=True
    )
    dbc = arrived.astype(f32).sum(axis=0)

    z_in = project(weights_zo)

    dt_low = dbc[:, :RANK].astype(bf16)
    delta_all = jax.nn.softplus(
        lax.dot_general(dt_low, dt_proj_w, contract_last, preferred_element_type=f32) + dt_bias
    ).reshape(steps, rows, -1)
    b_all = dbc[:, RANK : RANK + NSTATE].reshape(steps, rows, NSTATE)
    c_all = dbc[:, RANK + NSTATE :].reshape(steps, rows, NSTATE)
    decay = -jnp.exp(a_log)
    state = ssm_state
    gates = []
    for step in range(steps):
        delta = delta_all[step]
        act_real = acts[step].astype(f32)
        state = (
            jnp.exp(delta[:, None, :] * decay[None]) * state
            + (delta * act_real)[:, None, :] * b_all[step][:, :, None]
        )
        y_out = jnp.sum(c_all[step][:, :, None] * state, axis=1) + d_skip * act_real
        gates.append((y_out * jax.nn.silu(z_in[step].astype(f32))).astype(bf16))
    gated = jnp.concatenate(gates, axis=0)

    gated_chunks = [gated] + [from_x(gated, k) for k in (1, 2, 3)]
    away = from_partner(out_product(gated_chunks, weights_zo, 1 - yh, x, bf16))
    here = out_product(gated_chunks, weights_zo, yh, x, f32)
    block_out = (found.astype(f32) + (here + away.astype(f32))).astype(bf16).reshape(steps, rows, -1)
    return (in_new, out_new, block_out, window_state, state)


def solution(mesh):
    split = P(("fsdp", "chan"), None, None)
    flat = P(("fsdp", "chan"), None)
    placed = (
        split,
        split,
        split,
        split,
        flat,
        flat,
        flat,
        flat,
        P("fsdp", "chan"),
        P(None, "fsdp"),
        P("fsdp", None, "chan"),
        P("fsdp", None, "chan"),
        P(None, "chan"),
        P("chan"),
        P(None, "chan"),
        P("chan", None),
        P("chan"),
        P(None, "chan"),
        P("chan"),
    )
    return jax.shard_map(
        per_device,
        mesh=mesh,
        in_specs=placed,
        out_specs=(
            split,
            flat,
            P(None, "fsdp", "chan"),
            P("fsdp", None, "chan"),
            P("fsdp", None, "chan"),
        ),
        check_vma=False,
    )
```

```python
import functools
import math

import jax
import jax.numpy as jnp
from jax import lax
from jax.experimental import pallas as pl
from jax.experimental.pallas import tpu as pltpu
from jax.sharding import PartitionSpec as P

RANK = 256
NSTATE = 16

learn_rate = 0.01
beta_first = 0.8
beta_second = 0.95
adam_eps = 1e-08
weight_decay = 0.1
bias_first = 1.0 - math.pow(0.8, 10)
bias_second = 1.0 - math.pow(0.95, 10)
norm_eps = 1e-06

BOTH = ("fsdp", "chan")
DEVICES = [
    (yl, z, co, yh, x)
    for yl in range(2)
    for z in range(4)
    for co in range(2)
    for yh in range(2)
    for x in range(4)
]


def place_of(yl, z, co, yh, x):
    return (yl * 8 + z * 2 + co) * 8 + yh * 4 + x


def in_route(k):
    return [
        (place_of(yl, z, co, yh, x), place_of(yh, z, co, yl, (x + k) % 4))
        for yl, z, co, yh, x in DEVICES
    ]


def out_route(j):
    return [
        (place_of(yl, z, co, yh, x), place_of(yl, x, co, (yh + j) % 2, z))
        for yl, z, co, yh, x in DEVICES
    ]


def from_x(a, k):
    return lax.ppermute(a, "chan", [(i, (i // 4) * 4 + (i % 4 - k) % 4) for i in range(8)])


def from_partner(a):
    return lax.ppermute(a, "chan", [(i, i ^ 4) for i in range(8)])


def adam_update(master, moment, velocity, grad):
    gradient = grad.astype(jnp.float32)
    moment = beta_first * moment + (1.0 - beta_first) * gradient
    velocity = beta_second * velocity + (1.0 - beta_second) * gradient * gradient
    update = moment / bias_first / (jnp.sqrt(velocity / bias_second) + adam_eps)
    return master - learn_rate * (update + weight_decay * master)


def in_product_kernel(s_ref, a0, a1, a2, a3, w0, w1, o_ref, acc):
    k = pl.program_id(0)
    for kk, a in enumerate((a0, a1, a2, a3)):

        @pl.when(k == kk)
        def _(kk=kk, a=a):
            total = None
            for h, w in enumerate((w0, w1)):
                lhs = jnp.concatenate(
                    [a[:, h * 128 : h * 128 + 128], a[:, 256 + h * 128 : 384 + h * 128]], axis=1
                )
                part = jnp.dot(lhs, w[...].reshape(256, 512), preferred_element_type=jnp.float32)
                total = part if total is None else total + part
            if kk == 0:
                acc[...] = total
            elif kk < 3:
                acc[...] += total
            else:
                o_ref[...] = (acc[...] + total).astype(o_ref.dtype)


def in_product(chunks, weights, matrix, column, x, dtype):
    tokens = chunks[0].shape[0]
    scalars = jnp.stack([column, x]).astype(jnp.int32)
    whole = pl.BlockSpec((tokens, 512), lambda k, s: (0, 0))
    return pl.pallas_call(
        in_product_kernel,
        out_shape=jax.ShapeDtypeStruct((tokens, 512), dtype),
        grid_spec=pltpu.PrefetchScalarGridSpec(
            num_scalar_prefetch=1,
            grid=(4,),
            in_specs=[whole] * 4
            + [
                pl.BlockSpec((2, 128, 512), lambda k, s: (lax.rem(s[1] + k, 4), matrix, s[0])),
                pl.BlockSpec((2, 128, 512), lambda k, s: (4 + lax.rem(s[1] + k, 4), matrix, s[0])),
            ],
            out_specs=whole,
            scratch_shapes=[pltpu.VMEM((tokens, 512), jnp.float32)],
        ),
        compiler_params=pltpu.CompilerParams(vmem_limit_bytes=24 * 2**20),
        cost_estimate=pl.CostEstimate(
            flops=2 * tokens * 2048 * 512, bytes_accessed=6 * 2**20, transcendentals=0
        ),
        name="in_product",
    )(scalars, *chunks, weights, weights)


def out_product_kernel(s_ref, a0, a1, a2, a3, w_ref, o_ref, acc):
    k = pl.program_id(0)
    rows = [
        w_ref[xs * 2 + co, yh * 32 : yh * 32 + 32, :]
        for co in range(2)
        for yh in range(2)
        for xs in range(4)
    ]
    rhs = jnp.concatenate(rows, axis=0)
    for kk, a in enumerate((a0, a1, a2, a3)):

        @pl.when(k == kk)
        def _(kk=kk, a=a):
            total = lax.dot_general(
                a[...], rhs, (((1,), (1,)), ((), ())), preferred_element_type=jnp.float32
            )
            if kk == 0:
                acc[...] = total
            elif kk < 3:
                acc[...] += total
            else:
                o_ref[...] = (acc[...] + total).astype(o_ref.dtype)


def out_product(chunks, weights, block, x, dtype):
    tokens = chunks[0].shape[0]
    scalars = jnp.stack([block, x]).astype(jnp.int32)
    whole = pl.BlockSpec((tokens, 512), lambda k, s: (0, 0))

    def where(k, s):
        source = lax.rem(s[1] + k, 4)
        return (s[0], source // 2, lax.rem(source, 2))

    return pl.pallas_call(
        out_product_kernel,
        out_shape=jax.ShapeDtypeStruct((tokens, 512), dtype),
        grid_spec=pltpu.PrefetchScalarGridSpec(
            num_scalar_prefetch=1,
            grid=(4,),
            in_specs=[whole] * 4 + [pl.BlockSpec((8, 64, 512), where)],
            out_specs=whole,
            scratch_shapes=[pltpu.VMEM((tokens, 512), jnp.float32)],
        ),
        compiler_params=pltpu.CompilerParams(vmem_limit_bytes=24 * 2**20),
        cost_estimate=pl.CostEstimate(
            flops=2 * tokens * 2048 * 512, bytes_accessed=6 * 2**20, transcendentals=0
        ),
        name="out_product",
    )(scalars, *chunks, weights)


def per_device(
    in_master,
    in_moment,
    in_velocity,
    in_grad,
    out_master,
    out_moment,
    out_velocity,
    out_grad,
    embed_table,
    tokens,
    conv_state,
    ssm_state,
    conv_weight,
    conv_bias,
    x_proj_w,
    dt_proj_w,
    dt_bias,
    a_log,
    d_skip,
):
    bf16 = jnp.bfloat16
    f32 = jnp.float32
    chan = lax.axis_index("chan")
    yh, x = chan // 4, chan % 4
    replicas = lax.axis_size("fsdp")
    vocab_rows, feature_part = embed_table.shape
    steps, rows = tokens.shape
    count = steps * rows
    capacity = 2 * count // replicas

    flat_tokens = tokens.reshape(count)
    owner = flat_tokens // vocab_rows
    order = jnp.arange(count, dtype=jnp.int32)
    before = jnp.logical_and(owner[:, None] == owner[None, :], order[:, None] < order[None, :])
    slot = jnp.sum(before.astype(jnp.int32), axis=0)
    place = owner * capacity + slot
    slots = jnp.arange(replicas * capacity, dtype=jnp.int32)
    hit = place[None, :] == slots[:, None]
    requests = jnp.sum(jnp.where(hit, flat_tokens[None, :] + 1, 0), axis=1) - 1
    asked = lax.all_to_all(
        requests.reshape(replicas, capacity), "fsdp", split_axis=0, concat_axis=0, tiled=True
    )

    in_new = adam_update(in_master, in_moment, in_velocity, in_grad)
    out_new = adam_update(out_master, out_moment, out_velocity, out_grad)
    own = in_new.shape[0]

    blocks = jnp.moveaxis(in_new.astype(bf16), 1, 0).reshape(2, own, 2, 4, 512)
    pieces = [
        lax.dynamic_index_in_dim(blocks, (x + k) % 4, 3, keepdims=False).reshape(2, own, 1024)
        for k in range(4)
    ]
    *pieces, asked = lax.optimization_barrier((*pieces, asked))
    stacked = jnp.stack([lax.ppermute(pieces[k], BOTH, in_route(k)) for k in range(4)])
    weights_in = lax.all_gather(
        jnp.concatenate(
            [lax.dynamic_index_in_dim(stacked, (x - source) % 4, 0, keepdims=False) for source in range(4)],
            axis=1,
        ).reshape(8 * own, 1024),
        "fsdp",
        axis=0,
        tiled=False,
    )

    offset = jnp.clip(asked - lax.axis_index("fsdp") * vocab_rows, 0, vocab_rows - 1)
    looked = embed_table.at[offset.reshape(-1)].get(mode="promise_in_bounds")
    halves = out_new.astype(bf16).reshape(own, 2, 2048)
    sent = [lax.dynamic_index_in_dim(halves, (yh + j) % 2, 1, keepdims=False) for j in range(2)]
    *sent, looked = lax.optimization_barrier((*sent, looked))
    got = [lax.ppermute(sent[j], BOTH, out_route(j)) for j in range(2)]
    both = jnp.concatenate(
        [jnp.where(yh == 0, got[0], got[1]), jnp.where(yh == 0, got[1], got[0])], axis=0
    )
    weights_out = lax.all_gather(
        jnp.concatenate([both[:, :1024], both[:, 1024:]], axis=0), "fsdp", axis=0, tiled=False
    )
    replies = lax.all_to_all(
        looked.reshape(replicas, capacity, feature_part), "fsdp", split_axis=0, concat_axis=0, tiled=True
    )
    found = replies.reshape(replicas * capacity, feature_part).at[place].get(mode="promise_in_bounds")

    chunks = [found] + [from_x(found, k) for k in (1, 2, 3)]
    squares = sum(jnp.sum(jnp.square(c.astype(f32)), axis=1) for c in chunks).reshape(steps, rows)
    total_squares = squares + from_partner(squares)
    scale = lax.rsqrt(total_squares / (8 * feature_part) + norm_eps)

    def project(parts, matrix):
        away = from_partner(in_product(parts, weights_in, matrix, 1 - yh, x, bf16))
        here = in_product(parts, weights_in, matrix, yh, x, f32)
        total = (here + away.astype(f32)).reshape(steps, rows, -1)
        return (total * scale[:, :, None]).astype(bf16)

    x_in = project(chunks, 0)

    window = jnp.concatenate([conv_state, jnp.moveaxis(x_in, 0, 1)], axis=1)
    acts = []
    for step in range(steps):
        mixed_conv = (
            jnp.sum(window[:, step : step + 4].astype(f32) * conv_weight[None], axis=1) + conv_bias
        )
        acts.append(jax.nn.silu(mixed_conv).astype(bf16))
    window_state = window[:, steps:, :]
    act = jnp.concatenate(acts, axis=0)
    contract_last = (((1,), (1,)), ((), ()))
    partial_value = lax.dot_general(act, x_proj_w, contract_last, preferred_element_type=f32).astype(bf16)
    partials = partial_value.reshape(steps, rows, -1)
    *chunks_z, partials = lax.optimization_barrier((*chunks, partials))
    mine = lax.dynamic_index_in_dim(partials, x, 0, keepdims=False).astype(f32)
    for k in (1, 2, 3):
        piece = lax.dynamic_index_in_dim(partials, (x - k) % 4, 0, keepdims=False)
        mine = mine + from_x(piece, k).astype(f32)
    mine = (mine + from_partner(mine.astype(bf16)).astype(f32)).astype(bf16)
    shared = jnp.stack([mine] + [from_x(mine, k) for k in (1, 2, 3)])
    dbc = jnp.concatenate(
        [lax.dynamic_index_in_dim(shared, (s - x) % 4, 0, keepdims=False) for s in range(4)], axis=0
    ).astype(f32)

    z_in = project(chunks_z, 1)

    dt_low = dbc[:, :RANK].astype(bf16)
    delta_all = jax.nn.softplus(
        lax.dot_general(dt_low, dt_proj_w, contract_last, preferred_element_type=f32) + dt_bias
    ).reshape(steps, rows, -1)
    b_all = dbc[:, RANK : RANK + NSTATE].reshape(steps, rows, NSTATE)
    c_all = dbc[:, RANK + NSTATE :].reshape(steps, rows, NSTATE)
    decay = -jnp.exp(a_log)
    state = ssm_state
    gates = []
    for step in range(steps):
        delta = delta_all[step]
        act_real = acts[step].astype(f32)
        state = (
            jnp.exp(delta[:, None, :] * decay[None]) * state
            + (delta * act_real)[:, None, :] * b_all[step][:, :, None]
        )
        y_out = jnp.sum(c_all[step][:, :, None] * state, axis=1) + d_skip * act_real
        gates.append((y_out * jax.nn.silu(z_in[step].astype(f32))).astype(bf16))
    gated = jnp.concatenate(gates, axis=0)

    gated_chunks = [gated] + [from_x(gated, k) for k in (1, 2, 3)]
    away = from_partner(out_product(gated_chunks, weights_out, 1 - yh, x, bf16))
    here = out_product(gated_chunks, weights_out, yh, x, f32)
    block_out = (found.astype(f32) + (here + away.astype(f32))).astype(bf16).reshape(steps, rows, -1)
    return (in_new, out_new, block_out, window_state, state)


def solution(mesh):
    split = P(("fsdp", "chan"), None, None)
    flat = P(("fsdp", "chan"), None)
    placed = (
        split,
        split,
        split,
        split,
        flat,
        flat,
        flat,
        flat,
        P("fsdp", "chan"),
        P(None, "fsdp"),
        P("fsdp", None, "chan"),
        P("fsdp", None, "chan"),
        P(None, "chan"),
        P("chan"),
        P(None, "chan"),
        P("chan", None),
        P("chan"),
        P(None, "chan"),
        P("chan"),
    )
    return jax.shard_map(
        per_device,
        mesh=mesh,
        in_specs=placed,
        out_specs=(
            split,
            flat,
            P(None, "fsdp", "chan"),
            P("fsdp", None, "chan"),
            P("fsdp", None, "chan"),
        ),
        check_vma=False,
    )
```

```python
import functools
import math

import jax
import jax.numpy as jnp
from jax import lax
from jax.experimental import pallas as pl
from jax.experimental.pallas import tpu as pltpu
from jax.sharding import PartitionSpec as P

RANK = 256
NSTATE = 16

learn_rate = 0.01
beta_first = 0.8
beta_second = 0.95
adam_eps = 1e-08
weight_decay = 0.1
bias_first = 1.0 - math.pow(0.8, 10)
bias_second = 1.0 - math.pow(0.95, 10)
norm_eps = 1e-06

BOTH = ("fsdp", "chan")
PARTS = 1
DEVICES = [
    (yl, z, co, yh, x)
    for yl in range(2)
    for z in range(4)
    for co in range(2)
    for yh in range(2)
    for x in range(4)
]


def place_of(yl, z, co, yh, x):
    return (yl * 8 + z * 2 + co) * 8 + yh * 4 + x


def x_route(j, k):
    return [
        (place_of(yl, z, co, yh, x), place_of((yh + j) % 2, z, co, yl, (x + k) % 4))
        for yl, z, co, yh, x in DEVICES
    ]


def z_route(k):
    return x_route(0, k)


def out_route(j):
    return [
        (place_of(yl, z, co, yh, x), place_of(yl, x, co, (yh + j) % 2, z))
        for yl, z, co, yh, x in DEVICES
    ]


def from_x(a, k):
    return lax.ppermute(a, "chan", [(i, (i // 4) * 4 + (i % 4 - k) % 4) for i in range(8)])


def from_z(a, k):
    return lax.ppermute(
        a, "fsdp", [(i, (i // 8) * 8 + (i // 2 % 4 - k) % 4 * 2 + i % 2) for i in range(16)]
    )


def from_other_core(a):
    return lax.ppermute(a, "fsdp", [(i, i ^ 1) for i in range(16)])


def from_partner(a):
    return lax.ppermute(a, "chan", [(i, i ^ 4) for i in range(8)])


def adam_update(master, moment, velocity, grad):
    gradient = grad.astype(jnp.float32)
    moment = beta_first * moment + (1.0 - beta_first) * gradient
    velocity = beta_second * velocity + (1.0 - beta_second) * gradient * gradient
    update = moment / bias_first / (jnp.sqrt(velocity / bias_second) + adam_eps)
    return master - learn_rate * (update + weight_decay * master)


def adam_in_kernel(s_ref, master, moment, velocity, grad, new, send_x, send_z):
    for matrix, send in enumerate((send_x, send_z)):
        updated = adam_update(
            master[:, matrix, :], moment[:, matrix, :], velocity[:, matrix, :], grad[:, matrix, :]
        )
        new[:, matrix, :] = updated
        send[0] = updated.astype(send.dtype)


def adam_in(master, moment, velocity, grad, x):
    own = master.shape[0]
    block = pl.BlockSpec((own, 2, 512), lambda i, s: (0, 0, i))
    send = pl.BlockSpec((1, own, 512), lambda i, s: (lax.rem(lax.rem(i, 4) - s[0] + 4, 4), 0, i // 4))
    return pl.pallas_call(
        adam_in_kernel,
        out_shape=(
            jax.ShapeDtypeStruct(master.shape, jnp.float32),
            jax.ShapeDtypeStruct((4, own, 1024), jnp.bfloat16),
            jax.ShapeDtypeStruct((4, own, 1024), jnp.bfloat16),
        ),
        grid_spec=pltpu.PrefetchScalarGridSpec(
            num_scalar_prefetch=1,
            grid=(8,),
            in_specs=[block] * 4,
            out_specs=(block, send, send),
        ),
        cost_estimate=pl.CostEstimate(
            flops=20 * master.size, bytes_accessed=20 * master.size, transcendentals=master.size
        ),
        name="adam_in",
    )(x[None], master, moment, velocity, grad)


def x_rows(s_ref, own_ref, other_ref):
    x, yl, core = s_ref[1], s_ref[3], s_ref[4]
    halves = []
    for ref in (own_ref, other_ref):
        parts = []
        for yh in range(2):
            for source in range(4):
                at = lax.rem(yl - yh + 2, 2) * 4 + lax.rem(x - source + 4, 4)
                parts.append(ref[0, at])
        halves.append(jnp.concatenate(parts, axis=0))
    first = jnp.where(core == 0, halves[0], halves[1])
    second = jnp.where(core == 0, halves[1], halves[0])
    return first, second


def x_away_kernel(s_ref, a0, a1, a2, a3, own_ref, other_ref, o_ref, q_ref, acc, sq):
    k = pl.program_id(0)
    first, second = x_rows(s_ref, own_ref, other_ref)
    for kk, a in enumerate((a0, a1, a2, a3)):

        @pl.when(k == kk)
        def _(kk=kk, a=a):
            total = jnp.dot(a[:, :256], first, preferred_element_type=jnp.float32)
            total = total + jnp.dot(a[:, 256:], second, preferred_element_type=jnp.float32)
            real = a[...].astype(jnp.float32)
            square = jnp.sum(real * real, axis=1, keepdims=True)
            square = jnp.broadcast_to(square, sq.shape)
            if kk == 0:
                acc[...] = total
                sq[...] = square
            elif kk < 3:
                acc[...] += total
                sq[...] += square
            else:
                square = sq[...] + square
                q_ref[...] = square
                high = square.astype(jnp.bfloat16)
                low = (square - high.astype(jnp.float32)).astype(jnp.bfloat16)
                lane = lax.broadcasted_iota(jnp.int32, square.shape, 1)
                o_ref[:, :512] = (acc[...] + total).astype(o_ref.dtype)
                o_ref[:, 512:] = jnp.where(lane < 64, high.astype(jnp.float32), low.astype(jnp.float32)).astype(
                    o_ref.dtype
                )


def x_here_kernel(s_ref, a0, a1, a2, a3, own_ref, other_ref, o_ref, acc):
    k = pl.program_id(0)
    first, second = x_rows(s_ref, own_ref, other_ref)
    for kk, a in enumerate((a0, a1, a2, a3)):

        @pl.when(k == kk)
        def _(kk=kk, a=a):
            total = jnp.dot(a[:, :256], first, preferred_element_type=jnp.float32)
            total = total + jnp.dot(a[:, 256:], second, preferred_element_type=jnp.float32)
            if kk == 0:
                acc[...] = total
            elif kk < 3:
                acc[...] += total
            else:
                o_ref[...] = acc[...] + total


def x_product(chunks, own, other, scalars, away):
    tokens = chunks[0].shape[0]
    whole = pl.BlockSpec((tokens, 512), lambda k, s: (0, 0))
    weights = pl.BlockSpec((1, 8, 32, 512), lambda k, s: (lax.rem(s[1] + k - s[2] + 4, 4), 0, 0, s[0]))
    scratch = [pltpu.VMEM((tokens, 512), jnp.float32)]
    if away:
        out_shape = (
            jax.ShapeDtypeStruct((tokens, 640), jnp.bfloat16),
            jax.ShapeDtypeStruct((tokens, 128), jnp.float32),
        )
        out_specs = (
            pl.BlockSpec((tokens, 640), lambda k, s: (0, 0)),
            pl.BlockSpec((tokens, 128), lambda k, s: (0, 0)),
        )
        scratch = scratch + [pltpu.VMEM((tokens, 128), jnp.float32)]
    else:
        out_shape = jax.ShapeDtypeStruct((tokens, 512), jnp.float32)
        out_specs = whole
    return pl.pallas_call(
        x_away_kernel if away else x_here_kernel,
        out_shape=out_shape,
        grid_spec=pltpu.PrefetchScalarGridSpec(
            num_scalar_prefetch=1,
            grid=(4,),
            in_specs=[whole] * 4 + [weights, weights],
            out_specs=out_specs,
            scratch_shapes=scratch,
        ),
        compiler_params=pltpu.CompilerParams(vmem_limit_bytes=24 * 2**20),
        cost_estimate=pl.CostEstimate(
            flops=2 * tokens * 2048 * 512, bytes_accessed=6 * 2**20, transcendentals=0
        ),
        name="x_away" if away else "x_here",
    )(scalars, *chunks, own, other)


def conv_kernel(here, away, own_sq, window, weight, bias, proj, act, window_new, partial, scale):
    rows = window.shape[1]
    steps = here.shape[0] // rows
    sent = away[:, 512:].astype(jnp.float32)
    squares = own_sq[:, :1] + sent[:, :1] + sent[:, 64:65]
    factor = lax.rsqrt(squares / 4096.0 + norm_eps)
    scale[...] = jnp.broadcast_to(factor, scale.shape)
    taps = [window[t] for t in range(3)]
    for step in range(steps):
        at = slice(step * rows, (step + 1) * rows)
        total = here[at, :] + away[at, :512].astype(jnp.float32)
        taps.append((total * factor[at]).astype(jnp.bfloat16))
        mixed = taps[step].astype(jnp.float32) * weight[0:1, :]
        for t in range(1, 4):
            mixed = mixed + taps[step + t].astype(jnp.float32) * weight[t : t + 1, :]
        act[at, :] = jax.nn.silu(mixed + bias[...]).astype(jnp.bfloat16)
    for t in range(3):
        window_new[t] = taps[steps + t]
    partial[...] = lax.dot_general(
        act[...], proj[...], (((1,), (1,)), ((), ())), preferred_element_type=jnp.float32
    ).astype(jnp.bfloat16)


def conv(here, away, own_sq, window, weight, bias, proj):
    tokens = here.shape[0]
    return pl.pallas_call(
        conv_kernel,
        out_shape=(
            jax.ShapeDtypeStruct((tokens, 512), jnp.bfloat16),
            jax.ShapeDtypeStruct(window.shape, jnp.bfloat16),
            jax.ShapeDtypeStruct((tokens, proj.shape[0]), jnp.bfloat16),
            jax.ShapeDtypeStruct((tokens, 128), jnp.float32),
        ),
        compiler_params=pltpu.CompilerParams(vmem_limit_bytes=24 * 2**20),
        cost_estimate=pl.CostEstimate(
            flops=2 * tokens * 288 * 512, bytes_accessed=4 * 2**20, transcendentals=tokens * 512
        ),
        name="conv",
    )(here, away, own_sq, window, weight, bias, proj)


def in_product_kernel(s_ref, a0, a1, a2, a3, w0, w1, o_ref, acc):
    k = pl.program_id(0)
    for kk, a in enumerate((a0, a1, a2, a3)):

        @pl.when(k == kk)
        def _(kk=kk, a=a):
            total = None
            for h, w in enumerate((w0, w1)):
                lhs = jnp.concatenate(
                    [a[:, h * 128 : h * 128 + 128], a[:, 256 + h * 128 : 384 + h * 128]], axis=1
                )
                part = jnp.dot(lhs, w[...].reshape(256, 512), preferred_element_type=jnp.float32)
                total = part if total is None else total + part
            if kk == 0:
                acc[...] = total
            elif kk < 3:
                acc[...] += total
            else:
                o_ref[...] = (acc[...] + total).astype(o_ref.dtype)


def in_product(chunks, weights, matrix, column, x, dtype):
    tokens = chunks[0].shape[0]
    scalars = jnp.stack([column, x]).astype(jnp.int32)
    whole = pl.BlockSpec((tokens, 512), lambda k, s: (0, 0))
    return pl.pallas_call(
        in_product_kernel,
        out_shape=jax.ShapeDtypeStruct((tokens, 512), dtype),
        grid_spec=pltpu.PrefetchScalarGridSpec(
            num_scalar_prefetch=1,
            grid=(4,),
            in_specs=[whole] * 4
            + [
                pl.BlockSpec((2, 128, 512), lambda k, s: (lax.rem(s[1] + k, 4), matrix, s[0])),
                pl.BlockSpec((2, 128, 512), lambda k, s: (4 + lax.rem(s[1] + k, 4), matrix, s[0])),
            ],
            out_specs=whole,
            scratch_shapes=[pltpu.VMEM((tokens, 512), jnp.float32)],
        ),
        compiler_params=pltpu.CompilerParams(vmem_limit_bytes=24 * 2**20),
        cost_estimate=pl.CostEstimate(
            flops=2 * tokens * 2048 * 512, bytes_accessed=6 * 2**20, transcendentals=0
        ),
        name="in_product",
    )(scalars, *chunks, weights, weights)


def out_product_kernel(s_ref, a0, a1, a2, a3, w_ref, o_ref, acc):
    k = pl.program_id(0)
    rows = [
        w_ref[xs * 2 + co, yh * 32 : yh * 32 + 32, :]
        for co in range(2)
        for yh in range(2)
        for xs in range(4)
    ]
    rhs = jnp.concatenate(rows, axis=0)
    for kk, a in enumerate((a0, a1, a2, a3)):

        @pl.when(k == kk)
        def _(kk=kk, a=a):
            total = lax.dot_general(
                a[...], rhs, (((1,), (1,)), ((), ())), preferred_element_type=jnp.float32
            )
            if kk == 0:
                acc[...] = total
            elif kk < 3:
                acc[...] += total
            else:
                o_ref[...] = (acc[...] + total).astype(o_ref.dtype)


def out_product(chunks, weights, block, x, dtype):
    tokens = chunks[0].shape[0]
    scalars = jnp.stack([block, x]).astype(jnp.int32)
    whole = pl.BlockSpec((tokens, 512), lambda k, s: (0, 0))

    def where(k, s):
        source = lax.rem(s[1] + k, 4)
        return (s[0], 2 + source // 2, lax.rem(source, 2))

    return pl.pallas_call(
        out_product_kernel,
        out_shape=jax.ShapeDtypeStruct((tokens, 512), dtype),
        grid_spec=pltpu.PrefetchScalarGridSpec(
            num_scalar_prefetch=1,
            grid=(4,),
            in_specs=[whole] * 4 + [pl.BlockSpec((8, 64, 512), where)],
            out_specs=whole,
            scratch_shapes=[pltpu.VMEM((tokens, 512), jnp.float32)],
        ),
        compiler_params=pltpu.CompilerParams(vmem_limit_bytes=24 * 2**20),
        cost_estimate=pl.CostEstimate(
            flops=2 * tokens * 2048 * 512, bytes_accessed=6 * 2**20, transcendentals=0
        ),
        name="out_product",
    )(scalars, *chunks, weights)


def per_device(
    in_master,
    in_moment,
    in_velocity,
    in_grad,
    out_master,
    out_moment,
    out_velocity,
    out_grad,
    embed_table,
    tokens,
    conv_state,
    ssm_state,
    conv_weight,
    conv_bias,
    x_proj_w,
    dt_proj_w,
    dt_bias,
    a_log,
    d_skip,
):
    bf16 = jnp.bfloat16
    f32 = jnp.float32
    chan = lax.axis_index("chan")
    yh, x = chan // 4, chan % 4
    replicas = lax.axis_size("fsdp")
    vocab_rows, feature_part = embed_table.shape
    steps, rows = tokens.shape
    count = steps * rows
    capacity = 2 * count // replicas

    flat_tokens = tokens.reshape(count)
    owner = flat_tokens // vocab_rows
    order = jnp.arange(count, dtype=jnp.int32)
    before = jnp.logical_and(owner[:, None] == owner[None, :], order[:, None] < order[None, :])
    slot = jnp.sum(before.astype(jnp.int32), axis=0)
    place = owner * capacity + slot
    slots = jnp.arange(replicas * capacity, dtype=jnp.int32)
    hit = place[None, :] == slots[:, None]
    requests = jnp.sum(jnp.where(hit, flat_tokens[None, :] + 1, 0), axis=1) - 1
    asked = lax.all_to_all(
        requests.reshape(replicas, capacity), "fsdp", split_axis=0, concat_axis=0, tiled=True
    )

    fsdp = lax.axis_index("fsdp")
    yl, z, core = fsdp // 8, fsdp // 2 % 4, fsdp % 2
    own = in_master.shape[0]
    in_master, requests = lax.optimization_barrier((in_master, requests))
    in_new, pieces_x, pieces_z = adam_in(in_master, in_moment, in_velocity, in_grad, x)
    rows_x = jnp.stack([lax.ppermute(pieces_x[k], BOTH, x_route(j, k)) for j in range(2) for k in range(4)])

    out_new = adam_update(out_master, out_moment, out_velocity, out_grad)
    halves = out_new.astype(bf16).reshape(own, 2, 2048)
    sent = [lax.dynamic_index_in_dim(halves, (yh + j) % 2, 1, keepdims=False) for j in range(2)]
    rows_x, pieces_z, *sent, asked = lax.optimization_barrier((rows_x, pieces_z, *sent, asked))

    same_core = jnp.stack([rows_x] + [from_z(rows_x, k) for k in (1, 2, 3)])
    other_core = from_other_core(same_core)

    stacked = jnp.stack([lax.ppermute(pieces_z[k], BOTH, z_route(k)) for k in range(4)])
    rows_z = [lax.dynamic_index_in_dim(stacked, (x - source) % 4, 0, keepdims=False) for source in range(4)]
    got = [lax.ppermute(sent[j], BOTH, out_route(j)) for j in range(2)]
    both = jnp.concatenate(
        [jnp.where(yh == 0, got[0], got[1]), jnp.where(yh == 0, got[1], got[0])], axis=0
    )
    weights_zo = lax.all_gather(
        jnp.concatenate(rows_z + [both[:, :1024], both[:, 1024:]], axis=0), "fsdp", axis=0, tiled=False
    )

    offset = jnp.clip(asked - fsdp * vocab_rows, 0, vocab_rows - 1)
    looked = embed_table.at[offset.reshape(-1)].get(mode="promise_in_bounds")
    replies = lax.all_to_all(
        looked.reshape(replicas, capacity, feature_part), "fsdp", split_axis=0, concat_axis=0, tiled=True
    )
    found = replies.reshape(replicas * capacity, feature_part).at[place].get(mode="promise_in_bounds")

    decay = -jnp.exp(a_log)
    contract_last = (((1,), (1,)), ((), ()))
    state = ssm_state
    window = jnp.moveaxis(conv_state, 1, 0)
    scalars = jnp.stack([yh, x, z, yl, core]).astype(jnp.int32)
    scalars_away = jnp.stack([1 - yh, x, z, yl, core]).astype(jnp.int32)
    outs = []
    part_steps = steps // PARTS
    for part in range(PARTS):
        mine = found[part * part_steps * rows : (part + 1) * part_steps * rows]
        chunks = [mine] + [from_x(mine, k) for k in (1, 2, 3)]
        away, squares = x_product(chunks, same_core, other_core, scalars_away, True)
        away = from_partner(away)
        here = x_product(chunks, same_core, other_core, scalars, False)
        act, window, partial_value, scale = conv(
            here, away, squares, window, conv_weight, conv_bias[None], x_proj_w
        )

        partials = partial_value.reshape(4, -1, partial_value.shape[1])
        *chunks, partials = lax.optimization_barrier((*chunks, partials))
        quarter = lax.dynamic_index_in_dim(partials, x, 0, keepdims=False).astype(f32)
        for k in (1, 2, 3):
            piece = lax.dynamic_index_in_dim(partials, (x - k) % 4, 0, keepdims=False)
            quarter = quarter + from_x(piece, k).astype(f32)
        quarter = (quarter + from_partner(quarter.astype(bf16)).astype(f32)).astype(bf16)
        shared = jnp.stack([quarter] + [from_x(quarter, k) for k in (1, 2, 3)])
        dbc = jnp.concatenate(
            [lax.dynamic_index_in_dim(shared, (q - x) % 4, 0, keepdims=False) for q in range(4)], axis=0
        ).astype(f32)

        z_away = from_partner(in_product(chunks, weights_zo, 0, 1 - yh, x, bf16))
        z_here = in_product(chunks, weights_zo, 0, yh, x, f32)
        z_in = ((z_here + z_away.astype(f32)) * scale[:, :1]).astype(bf16)

        dt_low = dbc[:, :RANK].astype(bf16)
        delta_all = jax.nn.softplus(
            lax.dot_general(dt_low, dt_proj_w, contract_last, preferred_element_type=f32) + dt_bias
        )
        gates = []
        for step in range(part_steps):
            at = slice(step * rows, (step + 1) * rows)
            delta = delta_all[at]
            b_mat = dbc[at, RANK : RANK + NSTATE]
            c_mat = dbc[at, RANK + NSTATE :]
            act_real = act[at].astype(f32)
            state = (
                jnp.exp(delta[:, None, :] * decay[None]) * state
                + (delta * act_real)[:, None, :] * b_mat[:, :, None]
            )
            y_out = jnp.sum(c_mat[:, :, None] * state, axis=1) + d_skip * act_real
            gates.append((y_out * jax.nn.silu(z_in[at].astype(f32))).astype(bf16))
        gated = jnp.concatenate(gates, axis=0)

        gated_chunks = [gated] + [from_x(gated, k) for k in (1, 2, 3)]
        away = from_partner(out_product(gated_chunks, weights_zo, 1 - yh, x, bf16))
        here = out_product(gated_chunks, weights_zo, yh, x, f32)
        block = (mine.astype(f32) + (here + away.astype(f32))).astype(bf16)
        outs.append(block.reshape(part_steps, rows, -1))
    return (in_new, out_new, jnp.concatenate(outs, axis=0), jnp.moveaxis(window, 0, 1), state)


def solution(mesh):
    split = P(("fsdp", "chan"), None, None)
    flat = P(("fsdp", "chan"), None)
    placed = (
        split,
        split,
        split,
        split,
        flat,
        flat,
        flat,
        flat,
        P("fsdp", "chan"),
        P(None, "fsdp"),
        P("fsdp", None, "chan"),
        P("fsdp", None, "chan"),
        P(None, "chan"),
        P("chan"),
        P(None, "chan"),
        P("chan", None),
        P("chan"),
        P(None, "chan"),
        P("chan"),
    )
    return jax.shard_map(
        per_device,
        mesh=mesh,
        in_specs=placed,
        out_specs=(
            split,
            flat,
            P(None, "fsdp", "chan"),
            P("fsdp", None, "chan"),
            P("fsdp", None, "chan"),
        ),
        check_vma=False,
    )
```

```python
import functools
import math

import jax
import jax.numpy as jnp
from jax import lax
from jax.experimental import pallas as pl
from jax.experimental.pallas import tpu as pltpu
from jax.sharding import PartitionSpec as P

RANK = 256
NSTATE = 16

learn_rate = 0.01
beta_first = 0.8
beta_second = 0.95
adam_eps = 1e-08
weight_decay = 0.1
bias_first = 1.0 - math.pow(0.8, 10)
bias_second = 1.0 - math.pow(0.95, 10)
norm_eps = 1e-06

BOTH = ("fsdp", "chan")
PARTS = 2
DEVICES = [
    (yl, z, co, yh, x)
    for yl in range(2)
    for z in range(4)
    for co in range(2)
    for yh in range(2)
    for x in range(4)
]


def place_of(yl, z, co, yh, x):
    return (yl * 8 + z * 2 + co) * 8 + yh * 4 + x


def in_route(k):
    return [
        (place_of(yl, z, co, yh, x), place_of(yh, z, co, yl, (x + k) % 4))
        for yl, z, co, yh, x in DEVICES
    ]


def out_route(j):
    return [
        (place_of(yl, z, co, yh, x), place_of(yl, x, co, (yh + j) % 2, z))
        for yl, z, co, yh, x in DEVICES
    ]


def from_x(a, k):
    return lax.ppermute(a, "chan", [(i, (i // 4) * 4 + (i % 4 - k) % 4) for i in range(8)])


def from_partner(a):
    return lax.ppermute(a, "chan", [(i, i ^ 4) for i in range(8)])


IN_VMEM = pl.BlockSpec(memory_space=pltpu.VMEM)
IN_HBM = pl.BlockSpec(memory_space=pltpu.HBM)
IN_SMEM = pl.BlockSpec(memory_space=pltpu.SMEM)


def adam_update(master, moment, velocity, grad):
    gradient = grad.astype(jnp.float32)
    moment = beta_first * moment + (1.0 - beta_first) * gradient
    velocity = beta_second * velocity + (1.0 - beta_second) * gradient * gradient
    update = moment / bias_first / (jnp.sqrt(velocity / bias_second) + adam_eps)
    return master - learn_rate * (update + weight_decay * master)


def adam_in_kernel(s_ref, master, moment, velocity, grad, new, *rest):
    *sends, held = rest
    updated = adam_update(master[...], moment[...], velocity[...], grad[...])
    new[...] = updated
    held[...] = updated
    own = sends[0].shape[1]
    for k, send in enumerate(sends):
        at = lax.rem(s_ref[0] + k, 4) * 4
        for block in range(2):
            for tile in range(4):
                for matrix in range(2):
                    first = (block * 16 + at + tile) * 2 + matrix
                    rows = held[pl.ds(first, own, stride=64), :]
                    lanes = slice(block * 512 + tile * 128, block * 512 + tile * 128 + 128)
                    send[matrix, :, lanes] = rows.astype(jnp.bfloat16)


def tiles_of(a):
    return jnp.swapaxes(a.reshape(a.shape[0], 2, -1, 128), 1, 2).reshape(-1, 128)


def adam_in(master, moment, velocity, grad, x):
    own = master.shape[0]
    flat = (master.size // 128, 128)
    new, *sends = pl.pallas_call(
        adam_in_kernel,
        out_shape=(jax.ShapeDtypeStruct(flat, jnp.float32),)
        + (jax.ShapeDtypeStruct((2, own, 1024), jnp.bfloat16),) * 4,
        in_specs=[IN_SMEM] + [IN_VMEM] * 4,
        out_specs=(IN_VMEM,) * 5,
        scratch_shapes=[pltpu.VMEM(flat, jnp.float32)],
        compiler_params=pltpu.CompilerParams(vmem_limit_bytes=24 * 2**20),
        cost_estimate=pl.CostEstimate(
            flops=20 * master.size, bytes_accessed=20 * master.size, transcendentals=master.size
        ),
        name="adam_in",
    )(x[None], *(tiles_of(a) for a in (master, moment, velocity, grad)))
    new = jnp.swapaxes(new.reshape(own, -1, 2, 128), 1, 2).reshape(master.shape)
    return (new, *sends)


def conv_kernel(parts, here, *refs):
    aways, sums = refs[:parts], refs[parts : 2 * parts]
    window, weight, bias, proj, act, window_new, partial, scale = refs[2 * parts :]
    rows = window.shape[1]
    steps = here.shape[0] // rows
    taps = [window[t] for t in range(3)]
    for step in range(steps):
        at = slice(step * rows, (step + 1) * rows)
        p, local = divmod(step, steps // parts)
        inner = slice(local * rows, (local + 1) * rows)
        sent = aways[p][inner, 512:].astype(jnp.float32)
        squares = sums[p][inner, :1] + sent[:, :1] + sent[:, 64:65]
        factor = lax.rsqrt(squares / 4096.0 + norm_eps)
        scale[at, :] = jnp.broadcast_to(factor, (rows, 128))
        total = here[at, :] + aways[p][inner, :512].astype(jnp.float32)
        taps.append((total * factor).astype(jnp.bfloat16))
        mixed = taps[step].astype(jnp.float32) * weight[0:1, :]
        for t in range(1, 4):
            mixed = mixed + taps[step + t].astype(jnp.float32) * weight[t : t + 1, :]
        act[at, :] = jax.nn.silu(mixed + bias[...]).astype(jnp.bfloat16)
    for t in range(3):
        window_new[t] = taps[steps + t]
    partial[...] = lax.dot_general(
        act[...], proj[...], (((1,), (1,)), ((), ())), preferred_element_type=jnp.float32
    ).astype(jnp.bfloat16)


def conv(here, aways, sums, window, weight, bias, proj):
    tokens = here.shape[0]
    return pl.pallas_call(
        functools.partial(conv_kernel, len(aways)),
        out_shape=(
            jax.ShapeDtypeStruct((tokens, 512), jnp.bfloat16),
            jax.ShapeDtypeStruct(window.shape, jnp.bfloat16),
            jax.ShapeDtypeStruct((tokens, proj.shape[0]), jnp.bfloat16),
            jax.ShapeDtypeStruct((tokens, 128), jnp.float32),
        ),
        compiler_params=pltpu.CompilerParams(vmem_limit_bytes=24 * 2**20),
        cost_estimate=pl.CostEstimate(
            flops=2 * tokens * 288 * 512, bytes_accessed=4 * 2**20, transcendentals=tokens * 512
        ),
        name="conv",
    )(here, *aways, *sums, window, weight, bias, proj)


def in_product_kernel(parts, matrix, squared, s_ref, *refs):
    chunks, (w_ref, o_ref, *rest) = refs[: 4 * parts], refs[4 * parts :]
    held, acc, sems = rest[-3:]
    tokens = chunks[0].shape[0]
    column = pl.multiple_of(s_ref[0] * 512, 512)
    copies = []
    for k in range(4):
        for h in range(2):
            first = h * 8 + 2 * lax.rem(s_ref[1] + k, 4)
            copy = pltpu.make_async_copy(
                w_ref.at[pl.ds(first, 2), pl.ds(matrix * 128, 128), pl.ds(column, 512)],
                held.at[k, h],
                sems.at[k, h],
            )
            copy.start()
            copies.append(copy)
    for k in range(4):
        copies[2 * k].wait()
        copies[2 * k + 1].wait()
        rhs = held[k].reshape(512, 512)
        for p in range(parts):
            a = chunks[4 * p + k]
            at = slice(p * tokens, (p + 1) * tokens)
            lhs = jnp.concatenate([a[:, 0:128], a[:, 256:384], a[:, 128:256], a[:, 384:512]], axis=1)
            total = jnp.dot(lhs, rhs, preferred_element_type=jnp.float32)
            if k == 0:
                acc[at, :] = total
            elif k < 3:
                acc[at, :] += total
            else:
                o_ref[at, :512] = (acc[at, :] + total).astype(o_ref.dtype)
    if squared:
        q_ref = rest[0]
        for p in range(parts):
            at = slice(p * tokens, (p + 1) * tokens)
            squares = None
            for a in chunks[4 * p : 4 * p + 4]:
                real = a[...].astype(jnp.float32)
                squares = real * real if squares is None else squares + real * real
            square = jnp.broadcast_to(jnp.sum(squares, axis=1, keepdims=True), (tokens, 128))
            q_ref[at, :] = square
            high = square.astype(jnp.bfloat16).astype(jnp.float32)
            lane = lax.broadcasted_iota(jnp.int32, square.shape, 1)
            o_ref[at, 512:] = jnp.where(lane < 64, high, square - high).astype(o_ref.dtype)


def in_product(parts, weights, matrix, column, x, dtype, squared=False):
    tokens = parts[0][0].shape[0] * len(parts)
    scalars = jnp.stack([column, x]).astype(jnp.int32)
    out_shape = jax.ShapeDtypeStruct((tokens, 512), dtype)
    out_specs = IN_VMEM
    if squared:
        out_shape = (
            jax.ShapeDtypeStruct((tokens, 640), dtype),
            jax.ShapeDtypeStruct((tokens, 128), jnp.float32),
        )
        out_specs = (IN_VMEM, IN_VMEM)
    return pl.pallas_call(
        functools.partial(in_product_kernel, len(parts), matrix, squared),
        out_shape=out_shape,
        in_specs=[IN_SMEM] + [IN_VMEM] * (4 * len(parts)) + [IN_HBM],
        out_specs=out_specs,
        scratch_shapes=[
            pltpu.VMEM((4, 2, 2, 128, 512), jnp.bfloat16),
            pltpu.VMEM((tokens, 512), jnp.float32),
            pltpu.SemaphoreType.DMA((4, 2)),
        ],
        compiler_params=pltpu.CompilerParams(vmem_limit_bytes=24 * 2**20),
        cost_estimate=pl.CostEstimate(
            flops=2 * tokens * 2048 * 512, bytes_accessed=6 * 2**20, transcendentals=0
        ),
        name="in_product",
    )(scalars, *(c for part in parts for c in part), weights)


def out_product_kernel(parts, s_ref, *refs):
    chunks, (w_ref, o_ref, held, acc, sems) = refs[: 4 * parts], refs[4 * parts :]
    tokens = chunks[0].shape[0]
    copies = []
    for k in range(4):
        source = lax.rem(s_ref[1] + k, 4)
        rows = pl.multiple_of(source // 2 * 64, 64)
        columns = pl.multiple_of(lax.rem(source, 2) * 512, 512)
        copy = pltpu.make_async_copy(
            w_ref.at[pl.ds(s_ref[0] * 8, 8), pl.ds(rows, 64), pl.ds(columns, 512)], held.at[k], sems.at[k]
        )
        copy.start()
        copies.append(copy)
    for k in range(4):
        copies[k].wait()
        rows = [
            held[k, xs * 2 + co, yh * 32 : yh * 32 + 32, :]
            for co in range(2)
            for yh in range(2)
            for xs in range(4)
        ]
        rhs = jnp.concatenate(rows, axis=0)
        for p in range(parts):
            at = slice(p * tokens, (p + 1) * tokens)
            total = lax.dot_general(
                chunks[4 * p + k][...], rhs, (((1,), (1,)), ((), ())), preferred_element_type=jnp.float32
            )
            if k == 0:
                acc[at, :] = total
            elif k < 3:
                acc[at, :] += total
            else:
                o_ref[at, :] = (acc[at, :] + total).astype(o_ref.dtype)


def out_product(parts, weights, block, x, dtype):
    tokens = parts[0][0].shape[0] * len(parts)
    scalars = jnp.stack([block, x]).astype(jnp.int32)
    return pl.pallas_call(
        functools.partial(out_product_kernel, len(parts)),
        out_shape=jax.ShapeDtypeStruct((tokens, 512), dtype),
        in_specs=[IN_SMEM] + [IN_VMEM] * (4 * len(parts)) + [IN_HBM],
        out_specs=IN_VMEM,
        scratch_shapes=[
            pltpu.VMEM((4, 8, 64, 512), jnp.bfloat16),
            pltpu.VMEM((tokens, 512), jnp.float32),
            pltpu.SemaphoreType.DMA((4,)),
        ],
        compiler_params=pltpu.CompilerParams(vmem_limit_bytes=24 * 2**20),
        cost_estimate=pl.CostEstimate(
            flops=2 * tokens * 2048 * 512, bytes_accessed=6 * 2**20, transcendentals=0
        ),
        name="out_product",
    )(scalars, *(c for part in parts for c in part), weights)


def per_device(
    in_master,
    in_moment,
    in_velocity,
    in_grad,
    out_master,
    out_moment,
    out_velocity,
    out_grad,
    embed_table,
    tokens,
    conv_state,
    ssm_state,
    conv_weight,
    conv_bias,
    x_proj_w,
    dt_proj_w,
    dt_bias,
    a_log,
    d_skip,
):
    bf16 = jnp.bfloat16
    f32 = jnp.float32
    chan = lax.axis_index("chan")
    yh, x = chan // 4, chan % 4
    replicas = lax.axis_size("fsdp")
    vocab_rows, feature_part = embed_table.shape
    steps, rows = tokens.shape
    count = steps * rows
    capacity = 2 * count // replicas

    flat_tokens = tokens.reshape(count)
    owner = flat_tokens // vocab_rows
    order = jnp.arange(count, dtype=jnp.int32)
    before = jnp.logical_and(owner[:, None] == owner[None, :], order[:, None] < order[None, :])
    slot = jnp.sum(before.astype(jnp.int32), axis=0)
    place = owner * capacity + slot
    slots = jnp.arange(replicas * capacity, dtype=jnp.int32)
    hit = place[None, :] == slots[:, None]
    requests = jnp.sum(jnp.where(hit, flat_tokens[None, :] + 1, 0), axis=1) - 1
    in_master, requests = lax.optimization_barrier((in_master, requests))
    asked = lax.all_to_all(
        requests.reshape(replicas, capacity), "fsdp", split_axis=0, concat_axis=0, tiled=True
    )

    own = in_master.shape[0]
    in_new, *pieces = adam_in(in_master, in_moment, in_velocity, in_grad, x)
    first, second, third, fourth, asked = lax.optimization_barrier((*pieces, asked))
    rows_in = jnp.zeros((2, 4 * own, 1024), bf16)
    for k, piece in enumerate((first, second, third, fourth)):
        rows_in = lax.dynamic_update_slice(
            rows_in, lax.ppermute(piece, BOTH, in_route(k)), (0, (x - k) % 4 * own, 0)
        )
    weights_in = lax.all_gather(rows_in.reshape(8 * own, 1024), "fsdp", axis=0, tiled=False)

    offset = jnp.clip(asked - lax.axis_index("fsdp") * vocab_rows, 0, vocab_rows - 1)
    looked = embed_table.at[offset.reshape(-1)].get(mode="promise_in_bounds")
    replies = lax.all_to_all(
        looked.reshape(replicas, capacity, feature_part), "fsdp", split_axis=0, concat_axis=0, tiled=True
    )
    half = count // PARTS
    answers = replies.reshape(replicas * capacity, feature_part)
    found = [
        answers.at[place[p * half : (p + 1) * half]].get(mode="promise_in_bounds") for p in range(PARTS)
    ]

    def spread(parts):
        return [[part] + [from_x(part, k) for k in (1, 2, 3)] for part in parts]

    chunks = spread(found)
    aways, sums = [], []
    for part in chunks:
        away, squares = in_product([part], weights_in, 0, 1 - yh, x, bf16, squared=True)
        aways.append(away)
        sums.append(squares)
    out_new = adam_update(out_master, out_moment, out_velocity, out_grad)
    halves = out_new.astype(bf16).reshape(own, 2, 2048)
    sent = [lax.dynamic_index_in_dim(halves, (yh + j) % 2, 1, keepdims=False) for j in range(2)]
    last, sent0, sent1 = lax.optimization_barrier((aways[-1], *sent))
    aways = [from_partner(away) for away in (*aways[:-1], last)]
    got = [lax.ppermute(sent0, BOTH, out_route(0)), lax.ppermute(sent1, BOTH, out_route(1))]
    here = in_product(chunks, weights_in, 0, yh, x, f32)
    *flat_chunks, here = lax.optimization_barrier((*(c for part in chunks for c in part), here))
    chunks = [flat_chunks[4 * p : 4 * p + 4] for p in range(PARTS)]
    z_away = in_product(chunks, weights_in, 1, 1 - yh, x, bf16)
    z_here = in_product(chunks, weights_in, 1, yh, x, f32)
    act, window, partial_value, scale = conv(
        here, aways, sums, jnp.moveaxis(conv_state, 1, 0), conv_weight, conv_bias[None], x_proj_w
    )

    partials = partial_value.reshape(4, -1, partial_value.shape[1])
    partials, z_away, z_here, got0, got1 = lax.optimization_barrier((partials, z_away, z_here, *got))
    both = jnp.concatenate([jnp.where(yh == 0, got0, got1), jnp.where(yh == 0, got1, got0)], axis=0)
    rows_out = jnp.concatenate([both[:, :1024], both[:, 1024:]], axis=0)
    quarter = lax.dynamic_index_in_dim(partials, x, 0, keepdims=False).astype(f32)
    for k in (1, 2, 3):
        piece = lax.dynamic_index_in_dim(partials, (x - k) % 4, 0, keepdims=False)
        quarter = quarter + from_x(piece, k).astype(f32)
    quarter = (quarter + from_partner(quarter.astype(bf16)).astype(f32)).astype(bf16)
    z_away, quarter, rows_out = lax.optimization_barrier((z_away, quarter, rows_out))
    weights_out = lax.all_gather(rows_out, "fsdp", axis=0, tiled=False)
    shared = jnp.stack([quarter] + [from_x(quarter, k) for k in (1, 2, 3)])
    dbc = jnp.concatenate(
        [lax.dynamic_index_in_dim(shared, (q - x) % 4, 0, keepdims=False) for q in range(4)], axis=0
    ).astype(f32)

    z_away = from_partner(z_away)
    z_in = ((z_here + z_away.astype(f32)) * scale[:, :1]).astype(bf16)

    contract_last = (((1,), (1,)), ((), ()))
    dt_low = dbc[:, :RANK].astype(bf16)
    delta_all = jax.nn.softplus(
        lax.dot_general(dt_low, dt_proj_w, contract_last, preferred_element_type=f32) + dt_bias
    )
    decay = -jnp.exp(a_log)
    state = ssm_state
    gates = []
    for step in range(steps):
        at = slice(step * rows, (step + 1) * rows)
        delta = delta_all[at]
        b_mat = dbc[at, RANK : RANK + NSTATE]
        c_mat = dbc[at, RANK + NSTATE :]
        act_real = act[at].astype(f32)
        state = (
            jnp.exp(delta[:, None, :] * decay[None]) * state
            + (delta * act_real)[:, None, :] * b_mat[:, :, None]
        )
        y_out = jnp.sum(c_mat[:, :, None] * state, axis=1) + d_skip * act_real
        gates.append((y_out * jax.nn.silu(z_in[at].astype(f32))).astype(bf16))
    each = steps // PARTS
    gated = spread([jnp.concatenate(gates[p * each : (p + 1) * each], axis=0) for p in range(PARTS)])

    aways = [from_partner(out_product([part], weights_out, 1 - yh, x, bf16)) for part in gated]
    here = out_product(gated, weights_out, yh, x, f32)
    away = jnp.concatenate(aways, axis=0).astype(f32)
    rows_found = jnp.concatenate(found, axis=0).astype(f32)
    block_out = (rows_found + (here + away)).astype(bf16).reshape(steps, rows, -1)
    return (in_new, out_new, block_out, jnp.moveaxis(window, 0, 1), state)


def solution(mesh):
    split = P(("fsdp", "chan"), None, None)
    flat = P(("fsdp", "chan"), None)
    placed = (
        split,
        split,
        split,
        split,
        flat,
        flat,
        flat,
        flat,
        P("fsdp", "chan"),
        P(None, "fsdp"),
        P("fsdp", None, "chan"),
        P("fsdp", None, "chan"),
        P(None, "chan"),
        P("chan"),
        P(None, "chan"),
        P("chan", None),
        P("chan"),
        P(None, "chan"),
        P("chan"),
    )
    return jax.shard_map(
        per_device,
        mesh=mesh,
        in_specs=placed,
        out_specs=(
            split,
            flat,
            P(None, "fsdp", "chan"),
            P("fsdp", None, "chan"),
            P("fsdp", None, "chan"),
        ),
        check_vma=False,
    )
```

```python
import functools
import math

import jax
import jax.numpy as jnp
from jax import lax
from jax.experimental import pallas as pl
from jax.experimental.pallas import tpu as pltpu
from jax.sharding import PartitionSpec as P

RANK = 256
NSTATE = 16

learn_rate = 0.01
beta_first = 0.8
beta_second = 0.95
adam_eps = 1e-08
weight_decay = 0.1
bias_first = 1.0 - math.pow(0.8, 10)
bias_second = 1.0 - math.pow(0.95, 10)
norm_eps = 1e-06

BOTH = ("fsdp", "chan")
PARTS = 2
DEVICES = [
    (yl, z, co, yh, x)
    for yl in range(2)
    for z in range(4)
    for co in range(2)
    for yh in range(2)
    for x in range(4)
]


def place_of(yl, z, co, yh, x):
    return (yl * 8 + z * 2 + co) * 8 + yh * 4 + x


def in_route(k):
    return [
        (place_of(yl, z, co, yh, x), place_of(yh, z, co, yl, (x + k) % 4))
        for yl, z, co, yh, x in DEVICES
    ]


def out_route(j):
    return [
        (place_of(yl, z, co, yh, x), place_of(yl, x, co, (yh + j) % 2, z))
        for yl, z, co, yh, x in DEVICES
    ]


def from_x(a, k):
    return lax.ppermute(a, "chan", [(i, (i // 4) * 4 + (i % 4 - k) % 4) for i in range(8)])


def from_partner(a):
    return lax.ppermute(a, "chan", [(i, i ^ 4) for i in range(8)])


IN_VMEM = pl.BlockSpec(memory_space=pltpu.VMEM)
IN_HBM = pl.BlockSpec(memory_space=pltpu.HBM)
IN_SMEM = pl.BlockSpec(memory_space=pltpu.SMEM)


def in_hbm(a):
    return pltpu.with_memory_space_constraint(a, pltpu.HBM)


def adam_update(master, moment, velocity, grad):
    gradient = grad.astype(jnp.float32)
    moment = beta_first * moment + (1.0 - beta_first) * gradient
    velocity = beta_second * velocity + (1.0 - beta_second) * gradient * gradient
    update = moment / bias_first / (jnp.sqrt(velocity / bias_second) + adam_eps)
    return master - learn_rate * (update + weight_decay * master)


def adam_in_kernel(s_ref, master, moment, velocity, grad, new, *rest):
    *sends, held = rest
    updated = adam_update(master[...], moment[...], velocity[...], grad[...])
    new[...] = updated
    held[...] = updated
    own = sends[0].shape[1]
    for k, send in enumerate(sends):
        at = lax.rem(s_ref[0] + k, 4) * 4
        for block in range(2):
            for tile in range(4):
                for matrix in range(2):
                    first = (block * 16 + at + tile) * 2 + matrix
                    rows = held[pl.ds(first, own, stride=64), :]
                    lanes = slice(block * 512 + tile * 128, block * 512 + tile * 128 + 128)
                    send[matrix, :, lanes] = rows.astype(jnp.bfloat16)


def tiles_of(a):
    return jnp.swapaxes(a.reshape(a.shape[0], 2, -1, 128), 1, 2).reshape(-1, 128)


def adam_in(master, moment, velocity, grad, x):
    own = master.shape[0]
    flat = (master.size // 128, 128)
    new, *sends = pl.pallas_call(
        adam_in_kernel,
        out_shape=(jax.ShapeDtypeStruct(flat, jnp.float32),)
        + (jax.ShapeDtypeStruct((2, own, 1024), jnp.bfloat16),) * 4,
        in_specs=[IN_SMEM] + [IN_VMEM] * 4,
        out_specs=(IN_VMEM,) * 5,
        scratch_shapes=[pltpu.VMEM(flat, jnp.float32)],
        compiler_params=pltpu.CompilerParams(vmem_limit_bytes=24 * 2**20),
        cost_estimate=pl.CostEstimate(
            flops=20 * master.size, bytes_accessed=20 * master.size, transcendentals=master.size
        ),
        name="adam_in",
    )(x[None], *(tiles_of(a) for a in (master, moment, velocity, grad)))
    new = jnp.swapaxes(new.reshape(own, -1, 2, 128), 1, 2).reshape(master.shape)
    return (new, *sends)


def conv_kernel(parts, here, *refs):
    aways, sums = refs[:parts], refs[parts : 2 * parts]
    window, weight, bias, proj, act, window_new, partial, scale = refs[2 * parts :]
    rows = window.shape[1]
    steps = here.shape[0] // rows
    taps = [window[t] for t in range(3)]
    for step in range(steps):
        at = slice(step * rows, (step + 1) * rows)
        p, local = divmod(step, steps // parts)
        inner = slice(local * rows, (local + 1) * rows)
        sent = aways[p][inner, 512:].astype(jnp.float32)
        squares = sums[p][inner, :1] + sent[:, :1] + sent[:, 64:65]
        factor = lax.rsqrt(squares / 4096.0 + norm_eps)
        scale[at, :] = jnp.broadcast_to(factor, (rows, 128))
        total = here[at, :] + aways[p][inner, :512].astype(jnp.float32)
        taps.append((total * factor).astype(jnp.bfloat16))
        mixed = taps[step].astype(jnp.float32) * weight[0:1, :]
        for t in range(1, 4):
            mixed = mixed + taps[step + t].astype(jnp.float32) * weight[t : t + 1, :]
        act[at, :] = jax.nn.silu(mixed + bias[...]).astype(jnp.bfloat16)
    for t in range(3):
        window_new[t] = taps[steps + t]
    partial[...] = lax.dot_general(
        act[...], proj[...], (((1,), (1,)), ((), ())), preferred_element_type=jnp.float32
    ).astype(jnp.bfloat16)


def conv(here, aways, sums, window, weight, bias, proj):
    tokens = here.shape[0]
    return pl.pallas_call(
        functools.partial(conv_kernel, len(aways)),
        out_shape=(
            jax.ShapeDtypeStruct((tokens, 512), jnp.bfloat16),
            jax.ShapeDtypeStruct(window.shape, jnp.bfloat16),
            jax.ShapeDtypeStruct((tokens, proj.shape[0]), jnp.bfloat16),
            jax.ShapeDtypeStruct((tokens, 128), jnp.float32),
        ),
        compiler_params=pltpu.CompilerParams(vmem_limit_bytes=24 * 2**20),
        cost_estimate=pl.CostEstimate(
            flops=2 * tokens * 288 * 512, bytes_accessed=4 * 2**20, transcendentals=tokens * 512
        ),
        name="conv",
    )(here, *aways, *sums, window, weight, bias, proj)


def in_product_kernel(parts, matrix, squared, s_ref, *refs):
    chunks, (w_ref, o_ref, *rest) = refs[: 4 * parts], refs[4 * parts :]
    held, acc, sems = rest[-3:]
    tokens = chunks[0].shape[0]
    column = pl.multiple_of(s_ref[0] * 512, 512)
    copies = []
    for k in range(4):
        for h in range(2):
            first = h * 8 + 2 * lax.rem(s_ref[1] + k, 4)
            copy = pltpu.make_async_copy(
                w_ref.at[pl.ds(first, 2), pl.ds(matrix * 128, 128), pl.ds(column, 512)],
                held.at[k, h],
                sems.at[k, h],
            )
            copy.start()
            copies.append(copy)
    for k in range(4):
        copies[2 * k].wait()
        copies[2 * k + 1].wait()
        rhs = held[k].reshape(512, 512)
        for p in range(parts):
            a = chunks[4 * p + k]
            at = slice(p * tokens, (p + 1) * tokens)
            lhs = jnp.concatenate([a[:, 0:128], a[:, 256:384], a[:, 128:256], a[:, 384:512]], axis=1)
            total = jnp.dot(lhs, rhs, preferred_element_type=jnp.float32)
            if k == 0:
                acc[at, :] = total
            elif k < 3:
                acc[at, :] += total
            else:
                o_ref[at, :512] = (acc[at, :] + total).astype(o_ref.dtype)
    if squared:
        q_ref = rest[0]
        for p in range(parts):
            at = slice(p * tokens, (p + 1) * tokens)
            squares = None
            for a in chunks[4 * p : 4 * p + 4]:
                real = a[...].astype(jnp.float32)
                squares = real * real if squares is None else squares + real * real
            square = jnp.broadcast_to(jnp.sum(squares, axis=1, keepdims=True), (tokens, 128))
            q_ref[at, :] = square
            high = square.astype(jnp.bfloat16).astype(jnp.float32)
            lane = lax.broadcasted_iota(jnp.int32, square.shape, 1)
            o_ref[at, 512:] = jnp.where(lane < 64, high, square - high).astype(o_ref.dtype)


def in_product(parts, weights, matrix, column, x, dtype, squared=False):
    tokens = parts[0][0].shape[0] * len(parts)
    scalars = jnp.stack([column, x]).astype(jnp.int32)
    out_shape = jax.ShapeDtypeStruct((tokens, 512), dtype)
    out_specs = IN_VMEM
    if squared:
        out_shape = (
            jax.ShapeDtypeStruct((tokens, 640), dtype),
            jax.ShapeDtypeStruct((tokens, 128), jnp.float32),
        )
        out_specs = (IN_VMEM, IN_VMEM)
    return pl.pallas_call(
        functools.partial(in_product_kernel, len(parts), matrix, squared),
        out_shape=out_shape,
        in_specs=[IN_SMEM] + [IN_VMEM] * (4 * len(parts)) + [IN_HBM],
        out_specs=out_specs,
        scratch_shapes=[
            pltpu.VMEM((4, 2, 2, 128, 512), jnp.bfloat16),
            pltpu.VMEM((tokens, 512), jnp.float32),
            pltpu.SemaphoreType.DMA((4, 2)),
        ],
        compiler_params=pltpu.CompilerParams(vmem_limit_bytes=24 * 2**20),
        cost_estimate=pl.CostEstimate(
            flops=2 * tokens * 2048 * 512, bytes_accessed=6 * 2**20, transcendentals=0
        ),
        name="in_product",
    )(scalars, *(c for part in parts for c in part), weights)


def out_product_kernel(parts, s_ref, *refs):
    chunks, (w_ref, o_ref, held, acc, sems) = refs[: 4 * parts], refs[4 * parts :]
    tokens = chunks[0].shape[0]
    copies = []
    for k in range(4):
        source = lax.rem(s_ref[1] + k, 4)
        rows = pl.multiple_of(source // 2 * 64, 64)
        columns = pl.multiple_of(lax.rem(source, 2) * 512, 512)
        copy = pltpu.make_async_copy(
            w_ref.at[pl.ds(s_ref[0] * 8, 8), pl.ds(rows, 64), pl.ds(columns, 512)], held.at[k], sems.at[k]
        )
        copy.start()
        copies.append(copy)
    for k in range(4):
        copies[k].wait()
        rows = [
            held[k, xs * 2 + co, yh * 32 : yh * 32 + 32, :]
            for co in range(2)
            for yh in range(2)
            for xs in range(4)
        ]
        rhs = jnp.concatenate(rows, axis=0)
        for p in range(parts):
            at = slice(p * tokens, (p + 1) * tokens)
            total = lax.dot_general(
                chunks[4 * p + k][...], rhs, (((1,), (1,)), ((), ())), preferred_element_type=jnp.float32
            )
            if k == 0:
                acc[at, :] = total
            elif k < 3:
                acc[at, :] += total
            else:
                o_ref[at, :] = (acc[at, :] + total).astype(o_ref.dtype)


def out_product(parts, weights, block, x, dtype):
    tokens = parts[0][0].shape[0] * len(parts)
    scalars = jnp.stack([block, x]).astype(jnp.int32)
    return pl.pallas_call(
        functools.partial(out_product_kernel, len(parts)),
        out_shape=jax.ShapeDtypeStruct((tokens, 512), dtype),
        in_specs=[IN_SMEM] + [IN_VMEM] * (4 * len(parts)) + [IN_HBM],
        out_specs=IN_VMEM,
        scratch_shapes=[
            pltpu.VMEM((4, 8, 64, 512), jnp.bfloat16),
            pltpu.VMEM((tokens, 512), jnp.float32),
            pltpu.SemaphoreType.DMA((4,)),
        ],
        compiler_params=pltpu.CompilerParams(vmem_limit_bytes=24 * 2**20),
        cost_estimate=pl.CostEstimate(
            flops=2 * tokens * 2048 * 512, bytes_accessed=6 * 2**20, transcendentals=0
        ),
        name="out_product",
    )(scalars, *(c for part in parts for c in part), weights)


def per_device(
    in_master,
    in_moment,
    in_velocity,
    in_grad,
    out_master,
    out_moment,
    out_velocity,
    out_grad,
    embed_table,
    tokens,
    conv_state,
    ssm_state,
    conv_weight,
    conv_bias,
    x_proj_w,
    dt_proj_w,
    dt_bias,
    a_log,
    d_skip,
):
    bf16 = jnp.bfloat16
    f32 = jnp.float32
    chan = lax.axis_index("chan")
    yh, x = chan // 4, chan % 4
    replicas = lax.axis_size("fsdp")
    vocab_rows, feature_part = embed_table.shape
    steps, rows = tokens.shape
    count = steps * rows
    capacity = 2 * count // replicas

    flat_tokens = tokens.reshape(count)
    owner = flat_tokens // vocab_rows
    order = jnp.arange(count, dtype=jnp.int32)
    before = jnp.logical_and(owner[:, None] == owner[None, :], order[:, None] < order[None, :])
    slot = jnp.sum(before.astype(jnp.int32), axis=0)
    place = owner * capacity + slot
    slots = jnp.arange(replicas * capacity, dtype=jnp.int32)
    hit = place[None, :] == slots[:, None]
    requests = jnp.sum(jnp.where(hit, flat_tokens[None, :] + 1, 0), axis=1) - 1
    in_master, requests = lax.optimization_barrier((in_master, requests))
    asked = lax.all_to_all(
        requests.reshape(replicas, capacity), "fsdp", split_axis=0, concat_axis=0, tiled=True
    )

    own = in_master.shape[0]
    in_new, *pieces = adam_in(in_master, in_moment, in_velocity, in_grad, x)
    first, second, third, fourth, asked = lax.optimization_barrier((*pieces, asked))
    rows_in = jnp.zeros((2, 4 * own, 1024), bf16)
    for k, piece in enumerate((first, second, third, fourth)):
        rows_in = lax.dynamic_update_slice(
            rows_in, lax.ppermute(piece, BOTH, in_route(k)), (0, (x - k) % 4 * own, 0)
        )
    weights_in = in_hbm(lax.all_gather(rows_in.reshape(8 * own, 1024), "fsdp", axis=0, tiled=False))

    offset = jnp.clip(asked - lax.axis_index("fsdp") * vocab_rows, 0, vocab_rows - 1)
    looked = embed_table.at[offset.reshape(-1)].get(mode="promise_in_bounds")
    replies = lax.all_to_all(
        looked.reshape(replicas, capacity, feature_part), "fsdp", split_axis=0, concat_axis=0, tiled=True
    )
    half = count // PARTS
    answers = replies.reshape(replicas * capacity, feature_part)
    found = []
    wanted = place
    for p in range(PARTS):
        rows_p, wanted = lax.optimization_barrier(
            (answers.at[wanted[p * half : (p + 1) * half]].get(mode="promise_in_bounds"), wanted)
        )
        found.append(rows_p)

    def spread(parts):
        return [[part] + [from_x(part, k) for k in (1, 2, 3)] for part in parts]

    chunks = spread(found)
    aways, sums = [], []
    for part in chunks:
        away, squares = in_product([part], weights_in, 0, 1 - yh, x, bf16, squared=True)
        aways.append(away)
        sums.append(squares)
    out_new = adam_update(out_master, out_moment, out_velocity, out_grad)
    halves = out_new.astype(bf16).reshape(own, 2, 2048)
    sent = [lax.dynamic_index_in_dim(halves, (yh + j) % 2, 1, keepdims=False) for j in range(2)]
    last, sent0, sent1 = lax.optimization_barrier((aways[-1], *sent))
    aways = [from_partner(away) for away in (*aways[:-1], last)]
    got = [lax.ppermute(sent0, BOTH, out_route(0)), lax.ppermute(sent1, BOTH, out_route(1))]
    here = in_product(chunks, weights_in, 0, yh, x, f32)
    *flat_chunks, here = lax.optimization_barrier((*(c for part in chunks for c in part), here))
    chunks = [flat_chunks[4 * p : 4 * p + 4] for p in range(PARTS)]
    z_away = in_product(chunks, weights_in, 1, 1 - yh, x, bf16)
    z_here = in_product(chunks, weights_in, 1, yh, x, f32)
    act, window, partial_value, scale = conv(
        here, aways, sums, jnp.moveaxis(conv_state, 1, 0), conv_weight, conv_bias[None], x_proj_w
    )

    partials = partial_value.reshape(4, -1, partial_value.shape[1])
    partials, z_away, z_here, got0, got1 = lax.optimization_barrier((partials, z_away, z_here, *got))
    both = jnp.concatenate([jnp.where(yh == 0, got0, got1), jnp.where(yh == 0, got1, got0)], axis=0)
    rows_out = jnp.concatenate([both[:, :1024], both[:, 1024:]], axis=0)
    quarter = lax.dynamic_index_in_dim(partials, x, 0, keepdims=False).astype(f32)
    for k in (1, 2, 3):
        piece = lax.dynamic_index_in_dim(partials, (x - k) % 4, 0, keepdims=False)
        quarter = quarter + from_x(piece, k).astype(f32)
    quarter = (quarter + from_partner(quarter.astype(bf16)).astype(f32)).astype(bf16)
    z_away, quarter, rows_out = lax.optimization_barrier((z_away, quarter, rows_out))
    weights_out = in_hbm(lax.all_gather(rows_out, "fsdp", axis=0, tiled=False))
    shared = jnp.stack([quarter] + [from_x(quarter, k) for k in (1, 2, 3)])
    dbc = jnp.concatenate(
        [lax.dynamic_index_in_dim(shared, (q - x) % 4, 0, keepdims=False) for q in range(4)], axis=0
    ).astype(f32)

    z_away = from_partner(z_away)
    z_in = ((z_here + z_away.astype(f32)) * scale[:, :1]).astype(bf16)

    contract_last = (((1,), (1,)), ((), ()))
    dt_low = dbc[:, :RANK].astype(bf16)
    delta_all = jax.nn.softplus(
        lax.dot_general(dt_low, dt_proj_w, contract_last, preferred_element_type=f32) + dt_bias
    )
    decay = -jnp.exp(a_log)
    state = ssm_state
    gates = []
    for step in range(steps):
        at = slice(step * rows, (step + 1) * rows)
        delta = delta_all[at]
        b_mat = dbc[at, RANK : RANK + NSTATE]
        c_mat = dbc[at, RANK + NSTATE :]
        act_real = act[at].astype(f32)
        state = (
            jnp.exp(delta[:, None, :] * decay[None]) * state
            + (delta * act_real)[:, None, :] * b_mat[:, :, None]
        )
        y_out = jnp.sum(c_mat[:, :, None] * state, axis=1) + d_skip * act_real
        gates.append((y_out * jax.nn.silu(z_in[at].astype(f32))).astype(bf16))
    each = steps // PARTS
    gated = spread([jnp.concatenate(gates[p * each : (p + 1) * each], axis=0) for p in range(PARTS)])

    aways = [from_partner(out_product([part], weights_out, 1 - yh, x, bf16)) for part in gated]
    here = out_product(gated, weights_out, yh, x, f32)
    away = jnp.concatenate(aways, axis=0).astype(f32)
    rows_found = jnp.concatenate(found, axis=0).astype(f32)
    block_out = (rows_found + (here + away)).astype(bf16).reshape(steps, rows, -1)
    return (in_new, out_new, block_out, jnp.moveaxis(window, 0, 1), state)


def solution(mesh):
    split = P(("fsdp", "chan"), None, None)
    flat = P(("fsdp", "chan"), None)
    placed = (
        split,
        split,
        split,
        split,
        flat,
        flat,
        flat,
        flat,
        P("fsdp", "chan"),
        P(None, "fsdp"),
        P("fsdp", None, "chan"),
        P("fsdp", None, "chan"),
        P(None, "chan"),
        P("chan"),
        P(None, "chan"),
        P("chan", None),
        P("chan"),
        P(None, "chan"),
        P("chan"),
    )
    return jax.shard_map(
        per_device,
        mesh=mesh,
        in_specs=placed,
        out_specs=(
            split,
            flat,
            P(None, "fsdp", "chan"),
            P("fsdp", None, "chan"),
            P("fsdp", None, "chan"),
        ),
        check_vma=False,
    )
```

```python
import functools
import math

import jax
import jax.numpy as jnp
from jax import lax
from jax.experimental import pallas as pl
from jax.experimental.pallas import tpu as pltpu
from jax.sharding import PartitionSpec as P

RANK = 256
NSTATE = 16

learn_rate = 0.01
beta_first = 0.8
beta_second = 0.95
adam_eps = 1e-08
weight_decay = 0.1
bias_first = 1.0 - math.pow(0.8, 10)
bias_second = 1.0 - math.pow(0.95, 10)
norm_eps = 1e-06

BOTH = ("fsdp", "chan")
PARTS = 2
DEVICES = [
    (yl, z, co, yh, x)
    for yl in range(2)
    for z in range(4)
    for co in range(2)
    for yh in range(2)
    for x in range(4)
]


def place_of(yl, z, co, yh, x):
    return (yl * 8 + z * 2 + co) * 8 + yh * 4 + x


def in_route(k):
    return [
        (place_of(yl, z, co, yh, x), place_of(yh, z, co, yl, (x + k) % 4))
        for yl, z, co, yh, x in DEVICES
    ]


def out_route(j):
    return [
        (place_of(yl, z, co, yh, x), place_of(yl, x, co, (yh + j) % 2, z))
        for yl, z, co, yh, x in DEVICES
    ]


def from_x(a, k):
    return lax.ppermute(a, "chan", [(i, (i // 4) * 4 + (i % 4 - k) % 4) for i in range(8)])


def from_partner(a):
    return lax.ppermute(a, "chan", [(i, i ^ 4) for i in range(8)])


IN_VMEM = pl.BlockSpec(memory_space=pltpu.VMEM)
IN_HBM = pl.BlockSpec(memory_space=pltpu.HBM)
IN_SMEM = pl.BlockSpec(memory_space=pltpu.SMEM)


def in_hbm(a):
    return pltpu.with_memory_space_constraint(a, pltpu.HBM)


def adam_update(master, moment, velocity, grad):
    gradient = grad.astype(jnp.float32)
    moment = beta_first * moment + (1.0 - beta_first) * gradient
    velocity = beta_second * velocity + (1.0 - beta_second) * gradient * gradient
    update = moment / bias_first / (jnp.sqrt(velocity / bias_second) + adam_eps)
    return master - learn_rate * (update + weight_decay * master)


def adam_in_kernel(s_ref, master, moment, velocity, grad, new, *rest):
    *sends, held = rest
    updated = adam_update(master[...], moment[...], velocity[...], grad[...])
    new[...] = updated
    held[...] = updated
    own = sends[0].shape[1]
    for k, send in enumerate(sends):
        at = lax.rem(s_ref[0] + k, 4) * 4
        for block in range(2):
            for tile in range(4):
                for matrix in range(2):
                    first = (block * 16 + at + tile) * 2 + matrix
                    rows = held[pl.ds(first, own, stride=64), :]
                    lanes = slice(block * 512 + tile * 128, block * 512 + tile * 128 + 128)
                    send[matrix, :, lanes] = rows.astype(jnp.bfloat16)


def tiles_of(a):
    return jnp.swapaxes(a.reshape(a.shape[0], 2, -1, 128), 1, 2).reshape(-1, 128)


def adam_in(master, moment, velocity, grad, x):
    own = master.shape[0]
    flat = (master.size // 128, 128)
    new, *sends = pl.pallas_call(
        adam_in_kernel,
        out_shape=(jax.ShapeDtypeStruct(flat, jnp.float32),)
        + (jax.ShapeDtypeStruct((2, own, 1024), jnp.bfloat16),) * 4,
        in_specs=[IN_SMEM] + [IN_VMEM] * 4,
        out_specs=(IN_VMEM,) * 5,
        scratch_shapes=[pltpu.VMEM(flat, jnp.float32)],
        compiler_params=pltpu.CompilerParams(vmem_limit_bytes=24 * 2**20),
        cost_estimate=pl.CostEstimate(
            flops=20 * master.size, bytes_accessed=20 * master.size, transcendentals=master.size
        ),
        name="adam_in",
    )(x[None], *(tiles_of(a) for a in (master, moment, velocity, grad)))
    new = jnp.swapaxes(new.reshape(own, -1, 2, 128), 1, 2).reshape(master.shape)
    return (new, *sends)


def conv_kernel(parts, here, *refs):
    aways, sums = refs[:parts], refs[parts : 2 * parts]
    window, weight, bias, proj, act, window_new, partial, scale = refs[2 * parts :]
    rows = window.shape[1]
    steps = here.shape[0] // rows
    taps = [window[t] for t in range(3)]
    for step in range(steps):
        at = slice(step * rows, (step + 1) * rows)
        p, local = divmod(step, steps // parts)
        inner = slice(local * rows, (local + 1) * rows)
        squares = sums[p][inner, :1]
        factor = lax.rsqrt(squares / 4096.0 + norm_eps)
        scale[at, :] = jnp.broadcast_to(factor, (rows, 128))
        total = here[at, :] + aways[p][inner, :512].astype(jnp.float32)
        taps.append((total * factor).astype(jnp.bfloat16))
        mixed = taps[step].astype(jnp.float32) * weight[0:1, :]
        for t in range(1, 4):
            mixed = mixed + taps[step + t].astype(jnp.float32) * weight[t : t + 1, :]
        act[at, :] = jax.nn.silu(mixed + bias[...]).astype(jnp.bfloat16)
    for t in range(3):
        window_new[t] = taps[steps + t]
    partial[...] = lax.dot_general(
        act[...], proj[...], (((1,), (1,)), ((), ())), preferred_element_type=jnp.float32
    ).astype(jnp.bfloat16)


def conv(here, aways, sums, window, weight, bias, proj):
    tokens = here.shape[0]
    return pl.pallas_call(
        functools.partial(conv_kernel, len(aways)),
        out_shape=(
            jax.ShapeDtypeStruct((tokens, 512), jnp.bfloat16),
            jax.ShapeDtypeStruct(window.shape, jnp.bfloat16),
            jax.ShapeDtypeStruct((tokens, proj.shape[0]), jnp.bfloat16),
            jax.ShapeDtypeStruct((tokens, 128), jnp.float32),
        ),
        compiler_params=pltpu.CompilerParams(vmem_limit_bytes=24 * 2**20),
        cost_estimate=pl.CostEstimate(
            flops=2 * tokens * 288 * 512, bytes_accessed=4 * 2**20, transcendentals=tokens * 512
        ),
        name="conv",
    )(here, *aways, *sums, window, weight, bias, proj)


def in_product_kernel(parts, matrix, squared, s_ref, *refs):
    chunks, (w_ref, o_ref, *rest) = refs[: 4 * parts], refs[4 * parts :]
    held, acc, sems = rest[-3:]
    tokens = chunks[0].shape[0]
    column = pl.multiple_of(s_ref[0] * 512, 512)
    copies = []
    for k in range(4):
        for h in range(2):
            first = h * 8 + 2 * lax.rem(s_ref[1] + k, 4)
            copy = pltpu.make_async_copy(
                w_ref.at[pl.ds(first, 2), pl.ds(matrix * 128, 128), pl.ds(column, 512)],
                held.at[k, h],
                sems.at[k, h],
            )
            copy.start()
            copies.append(copy)
    for k in range(4):
        copies[2 * k].wait()
        copies[2 * k + 1].wait()
        rhs = held[k].reshape(512, 512)
        for p in range(parts):
            a = chunks[4 * p + k]
            at = slice(p * tokens, (p + 1) * tokens)
            lhs = jnp.concatenate([a[:, 0:128], a[:, 256:384], a[:, 128:256], a[:, 384:512]], axis=1)
            total = jnp.dot(lhs, rhs, preferred_element_type=jnp.float32)
            if k == 0:
                acc[at, :] = total
            elif k < 3:
                acc[at, :] += total
            else:
                o_ref[at, :512] = (acc[at, :] + total).astype(o_ref.dtype)
    if squared:
        q_ref = rest[0]
        for p in range(parts):
            at = slice(p * tokens, (p + 1) * tokens)
            squares = None
            for a in chunks[4 * p : 4 * p + 4]:
                real = a[...].astype(jnp.float32)
                squares = real * real if squares is None else squares + real * real
            square = jnp.broadcast_to(jnp.sum(squares, axis=1, keepdims=True), (tokens, 128))
            q_ref[at, :] = square
            high = square.astype(jnp.bfloat16).astype(jnp.float32)
            lane = lax.broadcasted_iota(jnp.int32, square.shape, 1)
            o_ref[at, 512:] = jnp.where(lane < 64, high, square - high).astype(o_ref.dtype)


def in_product(parts, weights, matrix, column, x, dtype, squared=False):
    tokens = parts[0][0].shape[0] * len(parts)
    scalars = jnp.stack([column, x]).astype(jnp.int32)
    out_shape = jax.ShapeDtypeStruct((tokens, 512), dtype)
    out_specs = IN_VMEM
    if squared:
        out_shape = (
            jax.ShapeDtypeStruct((tokens, 640), dtype),
            jax.ShapeDtypeStruct((tokens, 128), jnp.float32),
        )
        out_specs = (IN_VMEM, IN_VMEM)
    return pl.pallas_call(
        functools.partial(in_product_kernel, len(parts), matrix, squared),
        out_shape=out_shape,
        in_specs=[IN_SMEM] + [IN_VMEM] * (4 * len(parts)) + [IN_HBM],
        out_specs=out_specs,
        scratch_shapes=[
            pltpu.VMEM((4, 2, 2, 128, 512), jnp.bfloat16),
            pltpu.VMEM((tokens, 512), jnp.float32),
            pltpu.SemaphoreType.DMA((4, 2)),
        ],
        compiler_params=pltpu.CompilerParams(vmem_limit_bytes=24 * 2**20),
        cost_estimate=pl.CostEstimate(
            flops=2 * tokens * 2048 * 512, bytes_accessed=6 * 2**20, transcendentals=0
        ),
        name="in_product",
    )(scalars, *(c for part in parts for c in part), weights)


def out_product_kernel(parts, s_ref, *refs):
    chunks, (w_ref, o_ref, held, acc, sems) = refs[: 4 * parts], refs[4 * parts :]
    tokens = chunks[0].shape[0]
    copies = []
    for k in range(4):
        source = lax.rem(s_ref[1] + k, 4)
        rows = pl.multiple_of(source // 2 * 64, 64)
        columns = pl.multiple_of(lax.rem(source, 2) * 512, 512)
        copy = pltpu.make_async_copy(
            w_ref.at[pl.ds(s_ref[0] * 8, 8), pl.ds(rows, 64), pl.ds(columns, 512)], held.at[k], sems.at[k]
        )
        copy.start()
        copies.append(copy)
    for k in range(4):
        copies[k].wait()
        rows = [
            held[k, xs * 2 + co, yh * 32 : yh * 32 + 32, :]
            for co in range(2)
            for yh in range(2)
            for xs in range(4)
        ]
        rhs = jnp.concatenate(rows, axis=0)
        for p in range(parts):
            at = slice(p * tokens, (p + 1) * tokens)
            total = lax.dot_general(
                chunks[4 * p + k][...], rhs, (((1,), (1,)), ((), ())), preferred_element_type=jnp.float32
            )
            if k == 0:
                acc[at, :] = total
            elif k < 3:
                acc[at, :] += total
            else:
                o_ref[at, :] = (acc[at, :] + total).astype(o_ref.dtype)


def out_product(parts, weights, block, x, dtype):
    tokens = parts[0][0].shape[0] * len(parts)
    scalars = jnp.stack([block, x]).astype(jnp.int32)
    return pl.pallas_call(
        functools.partial(out_product_kernel, len(parts)),
        out_shape=jax.ShapeDtypeStruct((tokens, 512), dtype),
        in_specs=[IN_SMEM] + [IN_VMEM] * (4 * len(parts)) + [IN_HBM],
        out_specs=IN_VMEM,
        scratch_shapes=[
            pltpu.VMEM((4, 8, 64, 512), jnp.bfloat16),
            pltpu.VMEM((tokens, 512), jnp.float32),
            pltpu.SemaphoreType.DMA((4,)),
        ],
        compiler_params=pltpu.CompilerParams(vmem_limit_bytes=24 * 2**20),
        cost_estimate=pl.CostEstimate(
            flops=2 * tokens * 2048 * 512, bytes_accessed=6 * 2**20, transcendentals=0
        ),
        name="out_product",
    )(scalars, *(c for part in parts for c in part), weights)


def per_device(
    in_master,
    in_moment,
    in_velocity,
    in_grad,
    out_master,
    out_moment,
    out_velocity,
    out_grad,
    embed_table,
    tokens,
    conv_state,
    ssm_state,
    conv_weight,
    conv_bias,
    x_proj_w,
    dt_proj_w,
    dt_bias,
    a_log,
    d_skip,
):
    bf16 = jnp.bfloat16
    f32 = jnp.float32
    chan = lax.axis_index("chan")
    yh, x = chan // 4, chan % 4
    replicas = lax.axis_size("fsdp")
    vocab_rows, feature_part = embed_table.shape
    steps, rows = tokens.shape
    count = steps * rows
    capacity = 2 * count // replicas

    flat_tokens = tokens.reshape(count)
    owner = flat_tokens // vocab_rows
    order = jnp.arange(count, dtype=jnp.int32)
    before = jnp.logical_and(owner[:, None] == owner[None, :], order[:, None] < order[None, :])
    slot = jnp.sum(before.astype(jnp.int32), axis=0)
    place = owner * capacity + slot
    slots = jnp.arange(replicas * capacity, dtype=jnp.int32)
    hit = place[None, :] == slots[:, None]
    requests = jnp.sum(jnp.where(hit, flat_tokens[None, :] + 1, 0), axis=1) - 1
    in_master, requests = lax.optimization_barrier((in_master, requests))
    asked = lax.all_to_all(
        requests.reshape(replicas, capacity), "fsdp", split_axis=0, concat_axis=0, tiled=True
    )

    own = in_master.shape[0]
    in_new, *pieces = adam_in(in_master, in_moment, in_velocity, in_grad, x)
    first, second, third, fourth, asked = lax.optimization_barrier((*pieces, asked))
    rows_in = jnp.zeros((2, 4 * own, 1024), bf16)
    for k, piece in enumerate((first, second, third, fourth)):
        rows_in = lax.dynamic_update_slice(
            rows_in, lax.ppermute(piece, BOTH, in_route(k)), (0, (x - k) % 4 * own, 0)
        )
    weights_in = in_hbm(lax.all_gather(rows_in.reshape(8 * own, 1024), "fsdp", axis=0, tiled=False))

    offset = jnp.clip(asked - lax.axis_index("fsdp") * vocab_rows, 0, vocab_rows - 1)
    looked = embed_table.at[offset.reshape(-1)].get(mode="promise_in_bounds")
    replies = lax.all_to_all(
        looked.reshape(replicas, capacity, feature_part), "fsdp", split_axis=0, concat_axis=0, tiled=True
    )
    half = count // PARTS
    answers = replies.reshape(replicas * capacity, feature_part)
    found = []
    wanted = place
    for p in range(PARTS):
        rows_p, wanted = lax.optimization_barrier(
            (answers.at[wanted[p * half : (p + 1) * half]].get(mode="promise_in_bounds"), wanted)
        )
        found.append(rows_p)

    def spread(parts):
        return [[part] + [from_x(part, k) for k in (1, 2, 3)] for part in parts]

    chunks = spread(found)
    aways, sums = [], []
    for p, part in enumerate(chunks):
        squares = sum(jnp.sum(jnp.square(c.astype(f32)), axis=1) for c in part).reshape(-1, 128)
        squares = squares + from_partner(squares)
        *part, squares = lax.optimization_barrier((*part, squares))
        chunks[p] = part
        aways.append(in_product([part], weights_in, 0, 1 - yh, x, bf16))
        sums.append(jnp.broadcast_to(squares.reshape(-1, 1), (half, 128)))
    out_new = adam_update(out_master, out_moment, out_velocity, out_grad)
    halves = out_new.astype(bf16).reshape(own, 2, 2048)
    sent = [lax.dynamic_index_in_dim(halves, (yh + j) % 2, 1, keepdims=False) for j in range(2)]
    last, sent0, sent1 = lax.optimization_barrier((aways[-1], *sent))
    aways = [from_partner(away) for away in (*aways[:-1], last)]
    got = [lax.ppermute(sent0, BOTH, out_route(0)), lax.ppermute(sent1, BOTH, out_route(1))]
    here = in_product(chunks, weights_in, 0, yh, x, f32)
    *flat_chunks, here = lax.optimization_barrier((*(c for part in chunks for c in part), here))
    chunks = [flat_chunks[4 * p : 4 * p + 4] for p in range(PARTS)]
    z_away = in_product(chunks, weights_in, 1, 1 - yh, x, bf16)
    z_here = in_product(chunks, weights_in, 1, yh, x, f32)
    act, window, partial_value, scale = conv(
        here, aways, sums, jnp.moveaxis(conv_state, 1, 0), conv_weight, conv_bias[None], x_proj_w
    )

    partials = partial_value.reshape(4, -1, partial_value.shape[1])
    partials, z_away, z_here, got0, got1 = lax.optimization_barrier((partials, z_away, z_here, *got))
    both = jnp.concatenate([jnp.where(yh == 0, got0, got1), jnp.where(yh == 0, got1, got0)], axis=0)
    rows_out = jnp.concatenate([both[:, :1024], both[:, 1024:]], axis=0)
    quarter = lax.dynamic_index_in_dim(partials, x, 0, keepdims=False).astype(f32)
    for k in (1, 2, 3):
        piece = lax.dynamic_index_in_dim(partials, (x - k) % 4, 0, keepdims=False)
        quarter = quarter + from_x(piece, k).astype(f32)
    quarter = (quarter + from_partner(quarter.astype(bf16)).astype(f32)).astype(bf16)
    z_away, quarter, rows_out = lax.optimization_barrier((z_away, quarter, rows_out))
    weights_out = in_hbm(lax.all_gather(rows_out, "fsdp", axis=0, tiled=False))
    shared = jnp.stack([quarter] + [from_x(quarter, k) for k in (1, 2, 3)])
    dbc = jnp.concatenate(
        [lax.dynamic_index_in_dim(shared, (q - x) % 4, 0, keepdims=False) for q in range(4)], axis=0
    ).astype(f32)

    z_away = from_partner(z_away)
    z_in = ((z_here + z_away.astype(f32)) * scale[:, :1]).astype(bf16)

    contract_last = (((1,), (1,)), ((), ()))
    dt_low = dbc[:, :RANK].astype(bf16)
    delta_all = jax.nn.softplus(
        lax.dot_general(dt_low, dt_proj_w, contract_last, preferred_element_type=f32) + dt_bias
    )
    decay = -jnp.exp(a_log)
    state = ssm_state
    gates = []
    for step in range(steps):
        at = slice(step * rows, (step + 1) * rows)
        delta = delta_all[at]
        b_mat = dbc[at, RANK : RANK + NSTATE]
        c_mat = dbc[at, RANK + NSTATE :]
        act_real = act[at].astype(f32)
        state = (
            jnp.exp(delta[:, None, :] * decay[None]) * state
            + (delta * act_real)[:, None, :] * b_mat[:, :, None]
        )
        y_out = jnp.sum(c_mat[:, :, None] * state, axis=1) + d_skip * act_real
        gates.append((y_out * jax.nn.silu(z_in[at].astype(f32))).astype(bf16))
    each = steps // PARTS
    gated = spread([jnp.concatenate(gates[p * each : (p + 1) * each], axis=0) for p in range(PARTS)])

    aways = [from_partner(out_product([part], weights_out, 1 - yh, x, bf16)) for part in gated]
    here = out_product(gated, weights_out, yh, x, f32)
    away = jnp.concatenate(aways, axis=0).astype(f32)
    rows_found = jnp.concatenate(found, axis=0).astype(f32)
    block_out = (rows_found + (here + away)).astype(bf16).reshape(steps, rows, -1)
    return (in_new, out_new, block_out, jnp.moveaxis(window, 0, 1), state)


def solution(mesh):
    split = P(("fsdp", "chan"), None, None)
    flat = P(("fsdp", "chan"), None)
    placed = (
        split,
        split,
        split,
        split,
        flat,
        flat,
        flat,
        flat,
        P("fsdp", "chan"),
        P(None, "fsdp"),
        P("fsdp", None, "chan"),
        P("fsdp", None, "chan"),
        P(None, "chan"),
        P("chan"),
        P(None, "chan"),
        P("chan", None),
        P("chan"),
        P(None, "chan"),
        P("chan"),
    )
    return jax.shard_map(
        per_device,
        mesh=mesh,
        in_specs=placed,
        out_specs=(
            split,
            flat,
            P(None, "fsdp", "chan"),
            P("fsdp", None, "chan"),
            P("fsdp", None, "chan"),
        ),
        check_vma=False,
    )
```
